128 devices in a mesh: cell: 16 (over z, y_hi, core), vel: 8 (over y_lo, x).
Axes of the slice: x: 4, y: 4 (y_hi: 2, y_lo: 2; y = y_hi * 2 + y_lo), z: 4, core: 2. Of those that a mesh axis runs over, the one named last changes fastest.
Arguments:
- distribution: float32 [128, 128, 4096], P(None, 'cell', 'vel'), may hold values from 0.2 to 2
- cell_type: int32 [128, 128], P(None, 'cell'), may hold values from 0 to 2, as said below
- first_kernel: float32 [16, 4096], replicated, may hold values from -1.5 to 1.5
- second_kernel: float32 [16, 4096], replicated, may hold values from -1.5 to 1.5
- loss_kernel: float32 [4096], replicated, may hold values from -4 to 4
Outputs:
- updated: float32 [128, 128, 4096], P(None, 'cell', 'vel')
The draws below stay inside these ranges and needn't reach their ends.
Inputs may be any that keep to these rules, and one draw needn't show every extreme that they name: `cell_type`: cells with x = 0, x = 127 or y = 0 are 1, the other cells with y = 127 are 2, and every other cell is 1 with probability 1/40, else 0.
All inputs are finite; a program needn't handle non-finite values.
Results may differ from the reference program's by a relative error of at most 0.0004.
Values sent between devices are 32-bit elements; how exact they have to be, the bound alone decides.
A program may use at most 128 MiB of HBM per device.

```python
import math
import jax
import jax.numpy as jnp
from jax import lax

NVEL = 16
DIRS = 16
SLAB = 16
CY = 8
VEL = 4096
NX = 128
NY = 128
N_CELL = 16
N_VEL = 8


def mirror(values, axes):
    return jnp.roll(jnp.flip(values, axes), tuple((1 for axis_item in axes)), axes)


def draw_first_kernel(key, part):
    subkey = jax.random.fold_in(key, 11)
    raw = 0.3 * jax.random.normal(subkey, (DIRS, NVEL, NVEL, NVEL), jnp.float32)
    even = 0.5 * (raw + mirror(raw, (1, 2, 3)))
    return jnp.clip(even, -1.5, 1.5).reshape(DIRS, NVEL ** 3)


def draw_second_kernel(key, part):
    subkey = jax.random.fold_in(key, 12)
    raw = 0.3 * jax.random.normal(subkey, (DIRS, NVEL, NVEL, NVEL), jnp.float32)
    even = 0.5 * (raw + mirror(raw, (1, 2, 3)))
    return jnp.clip(even, -1.5, 1.5).reshape(DIRS, NVEL ** 3)


def draw_loss_kernel(key, part):
    subkey = jax.random.fold_in(key, 13)
    raw = jax.random.normal(subkey, (NVEL, NVEL, NVEL), jnp.float32)
    even = 0.5 * (raw + mirror(raw, (0, 1, 2)))
    return jnp.clip(even, -4.0, 4.0).reshape(NVEL ** 3)


def draw_cell_type(key, part):
    row_index = jnp.arange(NX, dtype=jnp.int32)[:, None]
    col_index = jnp.arange(NY, dtype=jnp.int32)[None, :]
    lottery = jax.random.randint(jax.random.fold_in(key, 14), (NX, NY), 0, 40)
    obstacle = jnp.where(lottery == 0, 1, 0)
    side_wall = (row_index == 0) | (row_index == NX - 1) | (col_index == 0)
    lid_cells = col_index == NY - 1
    return jnp.where(side_wall, 1, jnp.where(lid_cells, 2, obstacle)).astype(jnp.int32)


def steps_of(rng, shape, cuts, low, high):
    level = 1.0
    for axis_at, blocks in cuts:
        steps = jax.random.uniform(jax.random.fold_in(jax.random.fold_in(rng, 6), axis_at), (blocks,), jnp.float32, low / len(cuts), high / len(cuts))
        level = level * jnp.repeat(jnp.exp(steps), shape[axis_at] // blocks).reshape((-1,) + (1,) * (len(shape) - 1 - axis_at))
    return level


def setup_inputs(seed: int = 0) -> dict:
    splits = jax.random.split(jax.random.key(seed), 6)
    distribution = jnp.clip(jnp.exp(math.log(2.0) - 2.3025851 * jax.random.uniform(splits[0], (NX, NY, VEL), jnp.float32) ** steps_of(splits[0], (NX, NY, VEL), ((1, 16), (2, 8)), -0.2, 0.2)), 0.2, 2.0)
    cell_type = draw_cell_type(jax.random.fold_in(splits[5], 71), 0)
    first_kernel = draw_first_kernel(jax.random.fold_in(splits[5], 71), 0)
    second_kernel = draw_second_kernel(jax.random.fold_in(splits[5], 71), 0)
    loss_kernel = draw_loss_kernel(jax.random.fold_in(splits[5], 71), 0)
    return {"distribution": distribution, "cell_type": cell_type, "first_kernel": first_kernel, "second_kernel": second_kernel, "loss_kernel": loss_kernel}


courant = 0.45
collision_timestep = 0.1
pass_forms = ("ai,ijkc->ajkc", "aj,ijkc->iakc", "ak,ijkc->ijac")


def components(nvel):
    levels = (2.0 * jnp.arange(nvel, dtype=jnp.float32) - (nvel - 1)) / (nvel - 1)
    along_x = jnp.repeat(levels, nvel * nvel)
    along_y = jnp.tile(jnp.repeat(levels, nvel), nvel)
    along_z = jnp.tile(levels, nvel * nvel)
    return along_x, along_y, along_z


def wall_tables(along_x, along_y, along_z):
    still_wall = jnp.exp(-4.5 * (along_x * along_x + along_y * along_y + along_z * along_z))
    still_wall = still_wall / jnp.sum(still_wall)
    moving = jnp.exp(-0.5 * ((3.0 * along_x - 1.0) ** 2 + 9.0 * along_y * along_y + 9.0 * along_z * along_z))
    moving = moving / jnp.sum(moving)
    return still_wall, moving


def fourier_tables(nvel):
    indices = jnp.arange(nvel, dtype=jnp.int32)
    angles = 2.0 * math.pi * ((indices[:, None] * indices[None, :]) % nvel).astype(jnp.float32) / nvel
    cosine = jnp.cos(angles)
    sine_part = jnp.sin(angles)
    return (cosine.astype(jnp.bfloat16), (-sine_part).astype(jnp.bfloat16),
            (cosine / nvel).astype(jnp.bfloat16), (sine_part / nvel).astype(jnp.bfloat16))


def apply_table(matrix, operand, pattern):
    return jnp.einsum(pattern, matrix.astype(jnp.float32), operand.astype(jnp.float32), precision=lax.Precision.HIGHEST)


def real_pass(operand, cos_table, sin_table, pattern):
    return apply_table(cos_table, operand, pattern).astype(jnp.bfloat16), apply_table(sin_table, operand, pattern).astype(jnp.bfloat16)


def complex_pass(real_part, imag_part, cos_table, sin_table, pattern):
    new_real = apply_table(cos_table, real_part, pattern) - apply_table(sin_table, imag_part, pattern)
    new_imag = apply_table(cos_table, imag_part, pattern) + apply_table(sin_table, real_part, pattern)
    return new_real.astype(jnp.bfloat16), new_imag.astype(jnp.bfloat16)


def last_pass(real_part, imag_part, cos_table, sin_table, pattern):
    return apply_table(cos_table, real_part, pattern) - apply_table(sin_table, imag_part, pattern)


def spectrum_of(rounded, tables):
    real_part, imag_part = real_pass(rounded, tables[0], tables[1], pass_forms[0])
    real_part, imag_part = complex_pass(real_part, imag_part, tables[0], tables[1], pass_forms[1])
    return complex_pass(real_part, imag_part, tables[0], tables[1], pass_forms[2])


def inverse_of(kernel, spec_real, spec_imag, tables):
    weight = kernel[..., None]
    real_part = (weight * spec_real).astype(jnp.bfloat16)
    imag_part = (weight * spec_imag).astype(jnp.bfloat16)
    real_part, imag_part = complex_pass(real_part, imag_part, tables[2], tables[3], pass_forms[0])
    real_part, imag_part = complex_pass(real_part, imag_part, tables[2], tables[3], pass_forms[1])
    return last_pass(real_part, imag_part, tables[2], tables[3], pass_forms[2])


def collide(moved_block, kern_first, kern_second, kern_loss, tables):
    rounded = moved_block.astype(jnp.bfloat16)
    spec_real, spec_imag = spectrum_of(rounded, tables)

    def add_direction(direction, running):
        return running + inverse_of(kern_first[direction], spec_real, spec_imag, tables) * inverse_of(kern_second[direction], spec_real, spec_imag, tables)

    gain = lax.fori_loop(0, kern_first.shape[0], add_direction, jnp.zeros(moved_block.shape, jnp.float32))
    return gain - moved_block * inverse_of(kern_loss, spec_real, spec_imag, tables)


def transport(padded, along_x, along_y):
    center = padded[1:-1, 1:-1]
    back_x = center - padded[:-2, 1:-1]
    front_x = padded[2:, 1:-1] - center
    back_y = center - padded[1:-1, :-2]
    front_y = padded[1:-1, 2:] - center
    plus_x = jnp.maximum(along_x, 0.0)[None, None, :]
    minus_x = jnp.minimum(along_x, 0.0)[None, None, :]
    plus_y = jnp.maximum(along_y, 0.0)[None, None, :]
    minus_y = jnp.minimum(along_y, 0.0)[None, None, :]
    return -courant * (plus_x * back_x + minus_x * front_x + plus_y * back_y + minus_y * front_y)


def reference(distribution, cell_type, first_kernel, second_kernel, loss_kernel):
    vel_count = NVEL ** 3
    along_x, along_y, along_z = components(NVEL)
    still_wall, moving = wall_tables(along_x, along_y, along_z)
    density = jnp.sum(distribution, axis=2)
    fluid_cell_mask = cell_type == 0
    thermal = density[:, :, None] * jnp.where(cell_type[:, :, None] == 1, still_wall[None, None, :], moving[None, None, :])
    walled = jnp.where(fluid_cell_mask[:, :, None], distribution, thermal)
    padded = jnp.pad(walled, ((1, 1), (1, 1), (0, 0)))
    increment = transport(padded, along_x, along_y)
    advected_state = jnp.where(fluid_cell_mask[:, :, None], walled + increment, walled)
    tables = fourier_tables(NVEL)
    block_size = SLAB * CY
    block_count = N_VEL * N_CELL
    blocks = advected_state.reshape(N_VEL, SLAB, N_CELL, CY, vel_count).transpose(0, 2, 4, 1, 3)
    blocks = blocks.reshape(block_count, NVEL, NVEL, NVEL, block_size)
    kern_first = first_kernel.reshape(DIRS, NVEL, NVEL, NVEL)
    kern_second = second_kernel.reshape(DIRS, NVEL, NVEL, NVEL)
    kern_loss = loss_kernel.reshape(NVEL, NVEL, NVEL)

    def one_block(cell_piece):
        return collide(cell_piece, kern_first, kern_second, kern_loss, tables)

    result = lax.map(one_block, blocks)
    collision_operator = result.reshape(N_VEL, N_CELL, vel_count, SLAB, CY).transpose(0, 3, 1, 4, 2).reshape(NX, NY, vel_count)
    return jnp.where(fluid_cell_mask[:, :, None], advected_state + collision_timestep * collision_operator, advected_state)
```

```python
import functools

import jax
import jax.numpy as jnp
import numpy as np
from jax import lax
from jax.experimental import pallas as pl
from jax.experimental.pallas import tpu as pltpu
from jax.sharding import PartitionSpec as P

N = 16
DIRS = 16
courant = 0.45
collision_timestep = 0.1
NN = (((1,), (0,)), ((), ()))
NT = (((1,), (1,)), ((), ()))
F32 = jnp.float32
BF16 = jnp.bfloat16


def bf16_values(values):
    return np.asarray(values, np.float32).astype(BF16).astype(np.float64)


def line_tables():
    n = np.arange(N)
    angle = 2 * np.pi * (n[:, None] * n[None, :] % N) / N
    c, s = np.cos(angle), np.sin(angle)
    return bf16_values(c), bf16_values(-s), bf16_values(c / N), bf16_values(s / N)


def column_of(row, slot):
    if slot == 0:
        return row % 8, 0 if row < 8 else 8
    return row, slot


def j_table(fr, fi):
    eye = np.eye(N)
    real, imag = np.kron(fr, eye), np.kron(fi, eye)
    return np.block([[real, -imag], [imag, real]])


def k_tables(fr, fi):
    out = np.zeros((4, N, N, 2, N, N))
    for kind in range(4):
        for row in range(N):
            for slot in range(8):
                b, c = column_of(row, slot)
                if slot == 0 and b == 0 and kind in (0, 2):
                    first = 0 if kind == 0 else 8
                    out[kind, row, 0, 0, first] = fr[c]
                    out[kind, row, 8, 0, 8 - first] = fr[c]
                    continue
                if slot == 0 and b == 0 and kind == 3:
                    b = 8
                if kind < 3:
                    out[kind, row, slot, 0, b], out[kind, row, slot, 1, b] = fr[c], -fi[c]
                    out[kind, row, 8 + slot, 0, b], out[kind, row, 8 + slot, 1, b] = fi[c], fr[c]
                else:
                    m = (N - b) % N
                    out[kind, row, slot, 0, m], out[kind, row, slot, 1, m] = fr[c], fi[c]
                    out[kind, row, 8 + slot, 0, m], out[kind, row, 8 + slot, 1, m] = fi[c], -fr[c]
    return out.reshape(4, 256, 512)


def inverse_i_tables(ir, ii):
    out = np.zeros((2, N, N, N, N))
    for kind in range(2):
        for slot in range(8):
            im = 8 + slot
            if kind == 1 and slot == 0:
                out[1, :, 0, 0, 0], out[1, :, 0, 8, 8] = ir[:, 0], ir[:, 8]
                out[1, :, 8, 0, 8], out[1, :, 8, 8, 0] = ir[:, 0], ir[:, 8]
                for a in range(1, 8):
                    out[1, :, 0, a, 0], out[1, :, 0, a, 8] = 2 * ir[:, a], -2 * ii[:, a]
                    h = 8 + a
                    out[1, :, 8, h, 0], out[1, :, 8, h, 8] = 2 * ir[:, h], -2 * ii[:, h]
                continue
            out[kind, :, slot, :, slot], out[kind, :, slot, :, im] = ir, -ii
            out[kind, :, im, :, im], out[kind, :, im, :, slot] = ir, ii
    return out.reshape(2, 256, 256)


def inverse_jk_table(ir, ii):
    real = np.einsum("jb,kc->bcjk", ir, ir) - np.einsum("jb,kc->bcjk", ii, ii)
    imag = np.einsum("jb,kc->bcjk", ir, ii) + np.einsum("jb,kc->bcjk", ii, ir)
    out = np.zeros((N, N, N, N))
    for row in range(N):
        for slot in range(8):
            b, c = column_of(row, slot)
            if slot == 0 and b == 0:
                out[:, :, row, 0], out[:, :, row, 8] = real[0, c], real[8, c]
            else:
                out[:, :, row, slot], out[:, :, row, 8 + slot] = 2 * real[b, c], -2 * imag[b, c]
    return out.reshape(256, 256)


def packing_index():
    out = np.zeros((4, 2, 256), np.int32)
    for kind in range(4):
        for row in range(N):
            for slot in range(8):
                for part in range(2):
                    b, c = column_of(row, slot)
                    if slot == 0 and b == 0:
                        b = (8 * part, 0, 8 * (1 - part), 8)[kind]
                    place = row * 16 + 8 * part + slot
                    out[kind, 0, place] = b * 16 + c
                    out[kind, 1, place] = (N - b) % N * 16 + (N - c) % N
    return out


def kind_of(a):
    return 0 if a == 0 else 1 if a < 8 else 2 if a == 8 else 3


def pack_body(first_ref, second_ref, loss_ref, index_ref, out_ref, all_ref, mid_ref, table_ref):
    for kind in range(4):
        for side in range(2):
            source = lax.broadcasted_iota(jnp.int32, (256, 256), 0)
            hot = jnp.where(source == index_ref[kind, side : side + 1, :], 1.0, 0.0)
            table_ref[kind, side * 256 : side * 256 + 256, :] = hot.astype(BF16)
    all_ref[0:16] = first_ref[...]
    all_ref[16:32] = second_ref[...]
    all_ref[32:48] = jnp.broadcast_to(loss_ref[...], (16, 4096))
    for a in range(N):
        m = (N - a) % N
        x = jnp.concatenate(
            [all_ref[:, a * 256 : a * 256 + 256], all_ref[:, m * 256 : m * 256 + 256]], axis=1
        )
        high = x.astype(BF16)
        rest = x - high.astype(F32)
        mid = rest.astype(BF16)
        low = (rest - mid.astype(F32)).astype(BF16)
        parts = jnp.concatenate([high, mid, low], axis=0)
        o = lax.dot_general(parts, table_ref[kind_of(a)], NN, preferred_element_type=F32)
        mid_ref[a] = 0.5 * (o[0:48] + o[48:96] + o[96:144])
    for row in range(N):
        tile = slice(row // 8 * 128, row // 8 * 128 + 128)
        lane = lax.broadcasted_iota(jnp.int32, (48, 128), 1) // 16
        for half in range(2):
            total = jnp.zeros((48, 128), F32)
            for s in range(8):
                v = mid_ref[8 * half + s, :, tile]
                shift = (s - row) % 8 * 16
                v = pltpu.roll(v, shift, 1) if shift else v
                total = jnp.where(lane == s, v, total)
            out_ref[row, :, 128 * half : 128 * half + 128] = total


def pack_kernels(first, second, loss, table):
    return pl.pallas_call(
        pack_body,
        out_shape=jax.ShapeDtypeStruct((N, 48, 256), F32),
        scratch_shapes=[
            pltpu.VMEM((48, 4096), F32),
            pltpu.VMEM((N, 48, 256), F32),
            pltpu.VMEM((4, 512, 256), BF16),
        ],
        cost_estimate=pl.CostEstimate(flops=1 << 30, bytes_accessed=3 << 20, transcendentals=0),
        name="pack",
    )(first, second, loss.reshape(1, 4096), table)


def spectrum(load, jt_ref, kt_ref, x1_ref, x2_ref, sr_ref, s_ref, fr, fi):
    def rows(t, _):
        r = pl.ds(pl.multiple_of(t * 16, 16), 16)
        for half in range(2):
            x = [load(i, r, half).astype(BF16).astype(F32) for i in range(N)]
            even = [x[0]] + [x[n] + x[N - n] for n in range(1, 8)]
            odd = [None] + [x[n] - x[N - n] for n in range(1, 8)]
            lanes = slice(half * 128, half * 128 + 128)
            for a in range(9):
                re = even[0] + x[8] if a % 2 == 0 else even[0] - x[8]
                im = None
                for n in range(1, 8):
                    c, s = float(fr[a, n]), float(fi[a, n])
                    if abs(c) > 1e-6:
                        re = re + (even[n] * c if abs(c) < 1 else even[n] if c > 0 else -even[n])
                    if abs(s) > 1e-6:
                        term = odd[n] * s
                        im = term if im is None else im + term
                x1_ref[a, r, lanes] = re.astype(BF16)
                im = jnp.zeros_like(re) if im is None else im
                x1_ref[a, r, half * 128 + 256 : half * 128 + 384] = im.astype(BF16)
        return 0

    lax.fori_loop(0, 8, rows, 0)
    for a in range(9):
        o = lax.dot_general(jt_ref[...], x1_ref[a], NT, preferred_element_type=F32)
        x2_ref[a] = o.astype(BF16)
    for a in range(N):
        src = a if a <= 8 else N - a
        o = lax.dot_general(kt_ref[kind_of(a)], x2_ref[src], NN, preferred_element_type=F32)
        sr_ref[:, a * 16 : a * 16 + 16, :] = o.astype(BF16).reshape(N, 16, 128)
    for row in range(N):
        s_ref[row] = sr_ref[row].astype(F32).T


def collide_body(
    fr, fi, x_ref, fluid_ref, k_ref, jt_ref, kt_ref, ib_ref, ia_ref, out_ref,
    x1_ref, x2_ref, sr_ref, s_ref, z_ref, g_ref,
):
    def load(i, r, half):
        at = (i % 2) * 256 + half * 128
        return x_ref[i // 2, r, at : at + 128]

    spectrum(load, jt_ref, kt_ref, x1_ref, x2_ref, sr_ref, s_ref, fr, fi)
    g_ref[...] = jnp.zeros_like(g_ref)

    def direction(p, _):
        for row in range(N):
            s = s_ref[row]
            one = s * k_ref[row, pl.ds(p, 1), :]
            two = s * k_ref[row, pl.ds(16 + p, 1), :]
            both = jnp.concatenate([one.astype(BF16), two.astype(BF16)], axis=0)
            kind = 1 if row % 8 == 0 else 0
            o = lax.dot_general(ib_ref[kind], both, NT, preferred_element_type=F32)
            z_ref[:, row * 16 : row * 16 + 16, :] = o.astype(BF16).reshape(N, 16, 256)
        for i in range(N):
            o = lax.dot_general(ia_ref[...], z_ref[i], NN, preferred_element_type=F32)
            g_ref[i] += o[:, :128] * o[:, 128:]
        return 0

    lax.fori_loop(0, DIRS, direction, 0)
    for row in range(N):
        one = (s_ref[row] * k_ref[row, 32:33, :]).astype(BF16)
        kind = 1 if row % 8 == 0 else 0
        o = lax.dot_general(ib_ref[kind], one, NT, preferred_element_type=F32)
        z_ref[:, row * 16 : row * 16 + 16, :128] = o.astype(BF16).reshape(N, 16, 128)
    fluid = fluid_ref[...] == 0
    for i in range(N):
        loss = lax.dot_general(ia_ref[...], z_ref[i, :, :128], NN, preferred_element_type=F32)
        lanes = slice((i % 2) * 256, (i % 2) * 256 + 256)
        x = x_ref[i // 2, :, lanes]
        change = g_ref[i].T - x * loss.T
        out_ref[i // 2, :, lanes] = jnp.where(fluid, x + collision_timestep * change, x)


def constant_tables():
    fr, fi, ir, ii = line_tables()
    to = lambda t: np.asarray(t, np.float32).astype(BF16)
    return (fr, fi), tuple(
        to(t) for t in (j_table(fr, fi), k_tables(fr, fi), inverse_i_tables(ir, ii), inverse_jk_table(ir, ii))
    ), packing_index()


def collide(x, cells, packed, lines, tables):
    return pl.pallas_call(
        functools.partial(collide_body, *lines),
        out_shape=jax.ShapeDtypeStruct((8, 128, 512), F32),
        scratch_shapes=[
            pltpu.VMEM((9, 128, 512), BF16),
            pltpu.VMEM((9, 512, 128), BF16),
            pltpu.VMEM((N, 256, 128), BF16),
            pltpu.VMEM((N, 128, 256), F32),
            pltpu.VMEM((N, 256, 256), BF16),
            pltpu.VMEM((N, 256, 128), F32),
        ],
        compiler_params=pltpu.CompilerParams(vmem_limit_bytes=40 << 20),
        cost_estimate=pl.CostEstimate(flops=18 << 30, bytes_accessed=8 << 20, transcendentals=0),
        name="collide",
    )(x, cells, packed, *tables)


def components(nvel):
    levels = (2.0 * jnp.arange(nvel, dtype=F32) - (nvel - 1)) / (nvel - 1)
    along_x = jnp.repeat(levels, nvel * nvel)
    along_y = jnp.tile(jnp.repeat(levels, nvel), nvel)
    along_z = jnp.tile(levels, nvel * nvel)
    return along_x, along_y, along_z


def wall_tables(along_x, along_y, along_z):
    still_wall = jnp.exp(-4.5 * (along_x * along_x + along_y * along_y + along_z * along_z))
    still_wall = still_wall / jnp.sum(still_wall)
    moving = jnp.exp(
        -0.5 * ((3.0 * along_x - 1.0) ** 2 + 9.0 * along_y * along_y + 9.0 * along_z * along_z)
    )
    moving = moving / jnp.sum(moving)
    return still_wall, moving


def transport(padded, along_x, along_y):
    center = padded[1:-1, 1:-1]
    back_x = center - padded[:-2, 1:-1]
    front_x = padded[2:, 1:-1] - center
    back_y = center - padded[1:-1, :-2]
    front_y = padded[1:-1, 2:] - center
    plus_x = jnp.maximum(along_x, 0.0)[None, None, :]
    minus_x = jnp.minimum(along_x, 0.0)[None, None, :]
    plus_y = jnp.maximum(along_y, 0.0)[None, None, :]
    minus_y = jnp.minimum(along_y, 0.0)[None, None, :]
    return -courant * (plus_x * back_x + minus_x * front_x + plus_y * back_y + minus_y * front_y)


def on_device(lines, tables, one_hot, distribution, cell_type, first, second, loss):
    rows, cols, block = distribution.shape
    groups = lax.axis_size("vel")
    rank = lax.axis_index("vel")
    slab = rows // groups
    along_x, along_y, along_z = components(N)
    still, moving = wall_tables(along_x, along_y, along_z)
    here = lambda t: lax.dynamic_slice_in_dim(t, rank * block, block)
    partial = jnp.sum(distribution, axis=2)
    copies = lax.all_to_all(
        jnp.broadcast_to(partial[None], (groups, rows, cols)), "vel", 0, 0, tiled=True
    )
    density = jnp.sum(copies, axis=0)
    fluid = (cell_type == 0)[:, :, None]
    wall = jnp.where(cell_type[:, :, None] == 1, here(still)[None, None, :], here(moving)[None, None, :])
    walled = jnp.where(fluid, distribution, density[:, :, None] * wall)
    count = lax.axis_size("cell")
    up = [(i, i + 1) for i in range(count - 1)]
    below = lax.ppermute(walled[:, cols - 1 :], "cell", up)
    above = lax.ppermute(walled[:, :1], "cell", [(b, a) for a, b in up])
    rimmed = jnp.concatenate([below, walled, above], axis=1)
    padded = jnp.pad(rimmed, ((1, 1), (0, 0), (0, 0)))
    moved = jnp.where(fluid, walled + transport(padded, here(along_x), here(along_y)), walled)
    sent = lax.all_to_all(moved.reshape(groups, slab, cols, block), "vel", 0, 0, tiled=True)
    packed = pack_kernels(first, second, loss, one_hot)
    types = lax.dynamic_slice_in_dim(cell_type, rank * slab, slab, 0).reshape(slab * cols, 1)
    done = collide(sent.reshape(groups, slab * cols, block), types, packed, lines, tables)
    back = lax.all_to_all(done.reshape(groups, slab, cols, block), "vel", 0, 0, tiled=True)
    return back.reshape(rows, cols, block)


def solution(mesh):
    lines, tables, one_hot = constant_tables()

    def body(*arguments):
        return on_device(lines, tables, jnp.asarray(one_hot), *arguments)

    return jax.shard_map(
        body,
        mesh=mesh,
        in_specs=(P(None, "cell", "vel"), P(None, "cell"), P(), P(), P()),
        out_specs=P(None, "cell", "vel"),
        check_vma=False,
    )
```

```python
import functools

import jax
import jax.numpy as jnp
import numpy as np
from jax import lax
from jax.experimental import pallas as pl
from jax.experimental.pallas import tpu as pltpu
from jax.sharding import PartitionSpec as P

N = 16
DIRS = 16
courant = 0.45
collision_timestep = 0.1
NN = (((1,), (0,)), ((), ()))
NT = (((1,), (1,)), ((), ()))
F32 = jnp.float32
BF16 = jnp.bfloat16


def bf16_values(values):
    return np.asarray(values, np.float32).astype(BF16).astype(np.float64)


def line_tables():
    n = np.arange(N)
    angle = 2 * np.pi * (n[:, None] * n[None, :] % N) / N
    c, s = np.cos(angle), np.sin(angle)
    return bf16_values(c), bf16_values(-s), bf16_values(c / N), bf16_values(s / N)


def column_of(row, slot):
    if slot == 0:
        return row % 8, 0 if row < 8 else 8
    return row, slot


def j_table(fr, fi):
    eye = np.eye(N)
    real, imag = np.kron(fr, eye), np.kron(fi, eye)
    return np.block([[real, -imag], [imag, real]])


def k_tables(fr, fi):
    out = np.zeros((4, N, N, 2, N, N))
    for kind in range(4):
        for row in range(N):
            for slot in range(8):
                b, c = column_of(row, slot)
                if slot == 0 and b == 0 and kind in (0, 2):
                    first = 0 if kind == 0 else 8
                    out[kind, row, 0, 0, first] = fr[c]
                    out[kind, row, 8, 0, 8 - first] = fr[c]
                    continue
                if slot == 0 and b == 0 and kind == 3:
                    b = 8
                if kind < 3:
                    out[kind, row, slot, 0, b], out[kind, row, slot, 1, b] = fr[c], -fi[c]
                    out[kind, row, 8 + slot, 0, b], out[kind, row, 8 + slot, 1, b] = fi[c], fr[c]
                else:
                    m = (N - b) % N
                    out[kind, row, slot, 0, m], out[kind, row, slot, 1, m] = fr[c], fi[c]
                    out[kind, row, 8 + slot, 0, m], out[kind, row, 8 + slot, 1, m] = fi[c], -fr[c]
    return out.reshape(4, 256, 512)


def inverse_i_tables(ir, ii):
    out = np.zeros((2, N, N, N, N))
    for kind in range(2):
        for slot in range(8):
            im = 8 + slot
            if kind == 1 and slot == 0:
                out[1, :, 0, 0, 0], out[1, :, 0, 8, 8] = ir[:, 0], ir[:, 8]
                out[1, :, 8, 0, 8], out[1, :, 8, 8, 0] = ir[:, 0], ir[:, 8]
                for a in range(1, 8):
                    out[1, :, 0, a, 0], out[1, :, 0, a, 8] = 2 * ir[:, a], -2 * ii[:, a]
                    h = 8 + a
                    out[1, :, 8, h, 0], out[1, :, 8, h, 8] = 2 * ir[:, h], -2 * ii[:, h]
                continue
            out[kind, :, slot, :, slot], out[kind, :, slot, :, im] = ir, -ii
            out[kind, :, im, :, im], out[kind, :, im, :, slot] = ir, ii
    return out.reshape(2, 256, 256)


def inverse_jk_table(ir, ii):
    real = np.einsum("jb,kc->bcjk", ir, ir) - np.einsum("jb,kc->bcjk", ii, ii)
    imag = np.einsum("jb,kc->bcjk", ir, ii) + np.einsum("jb,kc->bcjk", ii, ir)
    out = np.zeros((N, N, N, N))
    for row in range(N):
        for slot in range(8):
            b, c = column_of(row, slot)
            if slot == 0 and b == 0:
                out[:, :, row, 0], out[:, :, row, 8] = real[0, c], real[8, c]
            else:
                out[:, :, row, slot], out[:, :, row, 8 + slot] = 2 * real[b, c], -2 * imag[b, c]
    return out.reshape(256, 256)


def packing_index():
    out = np.zeros((4, 2, 256), np.int32)
    for kind in range(4):
        for row in range(N):
            for slot in range(8):
                for part in range(2):
                    b, c = column_of(row, slot)
                    if slot == 0 and b == 0:
                        b = (8 * part, 0, 8 * (1 - part), 8)[kind]
                    place = row * 16 + 8 * part + slot
                    out[kind, 0, place] = b * 16 + c
                    out[kind, 1, place] = (N - b) % N * 16 + (N - c) % N
    return out


def kind_of(a):
    return 0 if a == 0 else 1 if a < 8 else 2 if a == 8 else 3


def pack(index_ref, all_ref, mid_ref, hot_ref, k_ref):
    for kind in range(4):
        for side in range(2):
            source = lax.broadcasted_iota(jnp.int32, (256, 256), 0)
            hot = jnp.where(source == index_ref[kind, side : side + 1, :], 1.0, 0.0)
            hot_ref[kind, side * 256 : side * 256 + 256, :] = hot.astype(BF16)
    for a in range(N):
        m = (N - a) % N
        x = jnp.concatenate(
            [all_ref[:, a * 256 : a * 256 + 256], all_ref[:, m * 256 : m * 256 + 256]], axis=1
        )
        high = x.astype(BF16)
        rest = x - high.astype(F32)
        mid = rest.astype(BF16)
        low = (rest - mid.astype(F32)).astype(BF16)
        parts = jnp.concatenate([high, mid, low], axis=0)
        o = lax.dot_general(parts, hot_ref[kind_of(a)], NN, preferred_element_type=F32)
        mid_ref[a] = 0.5 * (o[0:48] + o[48:96] + o[96:144])
    lane = lax.broadcasted_iota(jnp.int32, (48, 128), 1) // 16
    for row in range(N):
        tile = slice(row // 8 * 128, row // 8 * 128 + 128)
        for half in range(2):
            total = jnp.zeros((48, 128), F32)
            for s in range(8):
                v = mid_ref[8 * half + s, :, tile]
                shift = (s - row) % 8 * 16
                v = pltpu.roll(v, shift, 1) if shift else v
                total = jnp.where(lane == s, v, total)
            k_ref[row, :, 128 * half : 128 * half + 128] = total


ORDER = (1, 2, 3, 4, 5, 6, 7, 8, 0)


def spectrum(fr, fi, load, jt_ref, kt_ref, x1_ref, x2_ref, sr_ref, s_ref):
    def rows(t, _):
        r = pl.ds(pl.multiple_of(t * 16, 16), 16)
        for half in range(2):
            x = [load(i, r, half).astype(BF16).astype(F32) for i in range(N)]
            even = [x[0]] + [x[n] + x[N - n] for n in range(1, 8)]
            odd = [None] + [x[n] - x[N - n] for n in range(1, 8)]
            lanes = slice(half * 128, half * 128 + 128)
            for place, a in enumerate(ORDER):
                re = even[0] + x[8] if a % 2 == 0 else even[0] - x[8]
                im = None
                for n in range(1, 8):
                    c, s = float(fr[a, n]), float(fi[a, n])
                    if abs(c) > 1e-6:
                        re = re + (even[n] * c if abs(c) < 1 else even[n] if c > 0 else -even[n])
                    if abs(s) > 1e-6:
                        term = odd[n] * s
                        im = term if im is None else im + term
                im = jnp.zeros_like(re) if im is None else im
                at = pl.ds(pl.multiple_of(place * CELLS + t * 16, 16), 16)
                x1_ref[at, lanes] = re.astype(BF16)
                x1_ref[at, half * 128 + 256 : half * 128 + 384] = im.astype(BF16)
        return 0

    lax.fori_loop(0, CELLS // 16, rows, 0)
    wide = 4 * CELLS
    for first, size in ((0, wide), (wide, wide), (2 * wide, CELLS)):
        part = x1_ref[first : first + size, :]
        o = lax.dot_general(jt_ref[...], part, NT, preferred_element_type=F32)
        x2_ref[:, first : first + size] = o.astype(BF16)

    def put(kind, first, size, places):
        o = lax.dot_general(
            kt_ref[kind], x2_ref[:, first : first + size], NN, preferred_element_type=F32
        )
        for t, a in enumerate(places):
            v = o[:, t * CELLS : t * CELLS + CELLS].astype(BF16)
            sr_ref[:, a * 16 : a * 16 + 16, :] = v.reshape(N, 16, CELLS)

    put(1, 0, wide, (1, 2, 3, 4))
    put(3, 0, wide, (15, 14, 13, 12))
    put(1, wide, wide, (5, 6, 7))
    put(3, wide, wide, (11, 10, 9))
    put(2, wide + 3 * CELLS, CELLS, (8,))
    put(0, 2 * wide, CELLS, (0,))
    for row in range(N):
        s_ref[row] = sr_ref[row].astype(F32).T


CHUNKS = 2
CELLS = 128 // CHUNKS
GROUP = 8


def remote(src, dst, send, recv, peer):
    return pltpu.make_async_remote_copy(
        src_ref=src,
        dst_ref=dst,
        send_sem=send,
        recv_sem=recv,
        device_id={"vel": peer},
        device_id_type=pl.DeviceIdType.MESH,
    )


def step_body(
    fr, fi, moved_ref, fluid_ref, index_ref, first_ref, second_ref, loss_ref,
    jt_hbm, kt_hbm, ib_hbm, ia_hbm, out_ref,
    x_ref, r_ref, all_ref, mid_ref, hot_ref, k_ref, jt_ref, kt_ref, ib_ref, ia_ref,
    x1_ref, x2_ref, sr_ref, s_ref, z_ref, g_ref,
    send_sem, recv_sem, back_send, back_recv, own_sem, load_sem,
):
    me = lax.axis_index("vel")
    barrier = pltpu.get_barrier_semaphore()
    for s in range(1, GROUP):
        pl.semaphore_signal(
            barrier, inc=1, device_id={"vel": lax.rem(me + s, GROUP)},
            device_id_type=pl.DeviceIdType.MESH,
        )
    loads = [
        pltpu.make_async_copy(first_ref, all_ref.at[0:16], load_sem.at[0]),
        pltpu.make_async_copy(second_ref, all_ref.at[16:32], load_sem.at[1]),
        pltpu.make_async_copy(loss_ref, all_ref.at[32:40], load_sem.at[2]),
    ]
    tables = [
        pltpu.make_async_copy(jt_hbm, jt_ref, load_sem.at[3]),
        pltpu.make_async_copy(kt_hbm, kt_ref, load_sem.at[4]),
        pltpu.make_async_copy(ib_hbm, ib_ref, load_sem.at[5]),
        pltpu.make_async_copy(ia_hbm, ia_ref, load_sem.at[6]),
    ]
    own = [
        pltpu.make_async_copy(moved_ref.at[me, c], x_ref.at[c, me], own_sem.at[c])
        for c in range(CHUNKS)
    ]
    for copy in loads + tables + own:
        copy.start()
    pl.semaphore_wait(barrier, GROUP - 1)

    def send(c, s):
        peer = lax.rem(me + s, GROUP)
        return remote(
            moved_ref.at[peer, c], x_ref.at[c, me], send_sem.at[c, s], recv_sem.at[c, s], peer
        )

    def start(c):
        for s in range(1, GROUP):
            send(c, s).start()

    start(0)
    for copy in loads:
        copy.wait()
    all_ref[40:48] = jnp.zeros((8, 4096), F32)
    pack(index_ref, all_ref, mid_ref, hot_ref, k_ref)
    for copy in tables + own:
        copy.wait()
    for s in range(1, GROUP):
        send(0, s).wait_send()
    start(1)

    def chunk(c, _):
        for s in range(1, GROUP):
            send(c, s).wait_recv()

        def load(i, r, half):
            at = (i % 2) * 256 + half * 128
            return x_ref[c, i // 2, r, at : at + 128]

        spectrum(fr, fi, load, jt_ref, kt_ref, x1_ref, x2_ref, sr_ref, s_ref)
        g_ref[...] = jnp.zeros_like(g_ref)

        def directions(q, _):
            for row in range(N):
                s = s_ref[row]
                both = [
                    (s * k_ref[row, pl.ds(base + CHUNKS * q + t, 1), :]).astype(BF16)
                    for base in (0, 16)
                    for t in range(CHUNKS)
                ]
                kind = 1 if row % 8 == 0 else 0
                o = lax.dot_general(
                    ib_ref[kind], jnp.concatenate(both, axis=0), NT, preferred_element_type=F32
                )
                z_ref[:, row * 16 : row * 16 + 16, :] = o.astype(BF16).reshape(N, 16, 256)
            for i in range(N):
                o = lax.dot_general(ia_ref[...], z_ref[i], NN, preferred_element_type=F32)
                g_ref[i] += o[:, :128] * o[:, 128:]
            return 0

        lax.fori_loop(0, DIRS // CHUNKS, directions, 0)
        for row in range(N):
            one = (s_ref[row] * k_ref[row, 32:33, :]).astype(BF16)
            kind = 1 if row % 8 == 0 else 0
            o = lax.dot_general(ib_ref[kind], one, NT, preferred_element_type=F32)
            z_ref[:, row * 16 : row * 16 + 16, :CELLS] = o.astype(BF16).reshape(N, 16, CELLS)
        fluid = fluid_ref[c] == 0

        def finish(peer):
            for h in range(2):
                i = 2 * peer + h
                loss = lax.dot_general(
                    ia_ref[...], z_ref[i, :, :CELLS], NN, preferred_element_type=F32
                )
                gain = g_ref[i].T
                gain = gain[:CELLS] + gain[CELLS:]
                x = x_ref[c, peer, :, h * 256 : h * 256 + 256]
                change = gain - x * loss.T
                r_ref[c, peer, :, h * 256 : h * 256 + 256] = jnp.where(
                    fluid, x + collision_timestep * change, x
                )

        def one(s, _):
            peer = lax.rem(me + s, GROUP)
            finish(peer)
            back(c, s).start()
            return 0

        lax.fori_loop(1, GROUP, one, 0)
        finish(me)
        pltpu.make_async_copy(r_ref.at[c, me], out_ref.at[me, c], own_sem.at[c]).start()
        return 0

    def back(c, s):
        peer = lax.rem(me + s, GROUP)
        return remote(
            r_ref.at[c, peer], out_ref.at[me, c], back_send.at[c, s], back_recv.at[c, s], peer
        )

    lax.fori_loop(0, CHUNKS, chunk, 0)
    for c in range(CHUNKS):
        pltpu.make_async_copy(r_ref.at[c, me], out_ref.at[me, c], own_sem.at[c]).wait()
        for s in range(1, GROUP):
            if c:
                send(c, s).wait_send()
            back(c, s).wait()


def constant_tables():
    fr, fi, ir, ii = line_tables()
    to = lambda t: np.asarray(t, np.float32).astype(BF16)
    tables = (j_table(fr, fi), k_tables(fr, fi), inverse_i_tables(ir, ii), inverse_jk_table(ir, ii))
    return (fr, fi), tuple(to(t) for t in tables), packing_index()


def step(moved, types, index, first, second, loss, lines, tables):
    hbm = pl.BlockSpec(memory_space=pl.ANY)
    vmem = pl.BlockSpec(memory_space=pltpu.VMEM)
    dma = pltpu.SemaphoreType.DMA
    return pl.pallas_call(
        functools.partial(step_body, *lines),
        out_shape=jax.ShapeDtypeStruct(moved.shape, F32),
        in_specs=[hbm, vmem, vmem] + [hbm] * 7,
        out_specs=hbm,
        scratch_shapes=[
            pltpu.VMEM((CHUNKS, GROUP, CELLS, 512), F32),
            pltpu.VMEM((CHUNKS, GROUP, CELLS, 512), F32),
            pltpu.VMEM((48, 4096), F32),
            pltpu.VMEM((N, 48, 256), F32),
            pltpu.VMEM((4, 512, 256), BF16),
            pltpu.VMEM((N, 48, 256), F32),
            pltpu.VMEM((512, 512), BF16),
            pltpu.VMEM((4, 256, 512), BF16),
            pltpu.VMEM((2, 256, 256), BF16),
            pltpu.VMEM((256, 256), BF16),
            pltpu.VMEM((9 * CELLS, 512), BF16),
            pltpu.VMEM((512, 9 * CELLS), BF16),
            pltpu.VMEM((N, 256, CELLS), BF16),
            pltpu.VMEM((N, CELLS, 256), F32),
            pltpu.VMEM((N, 256, 256), BF16),
            pltpu.VMEM((N, 256, 128), F32),
            dma((CHUNKS, GROUP)),
            dma((CHUNKS, GROUP)),
            dma((CHUNKS, GROUP)),
            dma((CHUNKS, GROUP)),
            dma((CHUNKS,)),
            dma((7,)),
        ],
        compiler_params=pltpu.CompilerParams(
            vmem_limit_bytes=40 << 20, collective_id=0, has_side_effects=True
        ),
        name="step",
    )(moved, types, index, first, second, loss, *tables)


def components(nvel):
    levels = (2.0 * jnp.arange(nvel, dtype=F32) - (nvel - 1)) / (nvel - 1)
    along_x = jnp.repeat(levels, nvel * nvel)
    along_y = jnp.tile(jnp.repeat(levels, nvel), nvel)
    along_z = jnp.tile(levels, nvel * nvel)
    return along_x, along_y, along_z


def wall_tables(along_x, along_y, along_z):
    still_wall = jnp.exp(-4.5 * (along_x * along_x + along_y * along_y + along_z * along_z))
    still_wall = still_wall / jnp.sum(still_wall)
    moving = jnp.exp(
        -0.5 * ((3.0 * along_x - 1.0) ** 2 + 9.0 * along_y * along_y + 9.0 * along_z * along_z)
    )
    moving = moving / jnp.sum(moving)
    return still_wall, moving


def transport(padded, along_x, along_y):
    center = padded[1:-1, 1:-1]
    back_x = center - padded[:-2, 1:-1]
    front_x = padded[2:, 1:-1] - center
    back_y = center - padded[1:-1, :-2]
    front_y = padded[1:-1, 2:] - center
    plus_x = jnp.maximum(along_x, 0.0)[None, None, :]
    minus_x = jnp.minimum(along_x, 0.0)[None, None, :]
    plus_y = jnp.maximum(along_y, 0.0)[None, None, :]
    minus_y = jnp.minimum(along_y, 0.0)[None, None, :]
    return -courant * (plus_x * back_x + minus_x * front_x + plus_y * back_y + minus_y * front_y)


def on_device(lines, tables, one_hot, distribution, cell_type, first, second, loss):
    rows, cols, block = distribution.shape
    groups = lax.axis_size("vel")
    rank = lax.axis_index("vel")
    slab = rows // groups
    along_x, along_y, along_z = components(N)
    still, moving = wall_tables(along_x, along_y, along_z)
    here = lambda t: lax.dynamic_slice_in_dim(t, rank * block, block)
    partial = jnp.sum(distribution, axis=2)
    copies = lax.all_to_all(
        jnp.broadcast_to(partial[None], (groups, rows, cols)), "vel", 0, 0, tiled=True
    )
    density = jnp.sum(copies, axis=0)
    fluid = (cell_type == 0)[:, :, None]
    wall = jnp.where(cell_type[:, :, None] == 1, here(still)[None, None, :], here(moving)[None, None, :])
    walled = jnp.where(fluid, distribution, density[:, :, None] * wall)
    count = lax.axis_size("cell")
    up = [(i, i + 1) for i in range(count - 1)]
    below = lax.ppermute(walled[:, cols - 1 :], "cell", up)
    above = lax.ppermute(walled[:, :1], "cell", [(b, a) for a, b in up])
    rimmed = jnp.concatenate([below, walled, above], axis=1)
    padded = jnp.pad(rimmed, ((1, 1), (0, 0), (0, 0)))
    moved = jnp.where(fluid, walled + transport(padded, here(along_x), here(along_y)), walled)
    types = lax.dynamic_slice_in_dim(cell_type, rank * slab, slab, 0)
    done = step(
        moved.reshape(groups, CHUNKS, CELLS, block),
        types.reshape(CHUNKS, CELLS, 1),
        one_hot,
        first,
        second,
        jnp.broadcast_to(loss[None], (8, 4096)),
        lines,
        tables,
    )
    return done.reshape(rows, cols, block)


def solution(mesh):
    lines, tables, one_hot = constant_tables()

    def body(*arguments):
        return on_device(lines, tables, jnp.asarray(one_hot), *arguments)

    return jax.shard_map(
        body,
        mesh=mesh,
        in_specs=(P(None, "cell", "vel"), P(None, "cell"), P(), P(), P()),
        out_specs=P(None, "cell", "vel"),
        check_vma=False,
    )
```

```python
import functools

import jax
import jax.numpy as jnp
import numpy as np
from jax import lax
from jax.experimental import pallas as pl
from jax.experimental.pallas import tpu as pltpu
from jax.sharding import PartitionSpec as P

N = 16
DIRS = 16
courant = 0.45
collision_timestep = 0.1
NN = (((1,), (0,)), ((), ()))
NT = (((1,), (1,)), ((), ()))
F32 = jnp.float32
BF16 = jnp.bfloat16


def bf16_values(values):
    return np.asarray(values, np.float32).astype(BF16).astype(np.float64)


def line_tables():
    n = np.arange(N)
    angle = 2 * np.pi * (n[:, None] * n[None, :] % N) / N
    c, s = np.cos(angle), np.sin(angle)
    return bf16_values(c), bf16_values(-s), bf16_values(c / N), bf16_values(s / N)


def column_of(row, slot):
    if slot == 0:
        return row % 8, 0 if row < 8 else 8
    return row, slot


def j_table(fr, fi):
    eye = np.eye(N)
    real, imag = np.kron(fr, eye), np.kron(fi, eye)
    return np.block([[real, -imag], [imag, real]])


def k_tables(fr, fi):
    out = np.zeros((4, N, N, 2, N, N))
    for kind in range(4):
        for row in range(N):
            for slot in range(8):
                b, c = column_of(row, slot)
                if slot == 0 and b == 0 and kind in (0, 2):
                    first = 0 if kind == 0 else 8
                    out[kind, row, 0, 0, first] = fr[c]
                    out[kind, row, 8, 0, 8 - first] = fr[c]
                    continue
                if slot == 0 and b == 0 and kind == 3:
                    b = 8
                if kind < 3:
                    out[kind, row, slot, 0, b], out[kind, row, slot, 1, b] = fr[c], -fi[c]
                    out[kind, row, 8 + slot, 0, b], out[kind, row, 8 + slot, 1, b] = fi[c], fr[c]
                else:
                    m = (N - b) % N
                    out[kind, row, slot, 0, m], out[kind, row, slot, 1, m] = fr[c], fi[c]
                    out[kind, row, 8 + slot, 0, m], out[kind, row, 8 + slot, 1, m] = fi[c], -fr[c]
    return out.reshape(4, 256, 512)


def inverse_i_tables(ir, ii):
    out = np.zeros((2, N, N, N, N))
    for kind in range(2):
        for slot in range(8):
            im = 8 + slot
            if kind == 1 and slot == 0:
                out[1, :, 0, 0, 0], out[1, :, 0, 8, 8] = ir[:, 0], ir[:, 8]
                out[1, :, 8, 0, 8], out[1, :, 8, 8, 0] = ir[:, 0], ir[:, 8]
                for a in range(1, 8):
                    out[1, :, 0, a, 0], out[1, :, 0, a, 8] = 2 * ir[:, a], -2 * ii[:, a]
                    h = 8 + a
                    out[1, :, 8, h, 0], out[1, :, 8, h, 8] = 2 * ir[:, h], -2 * ii[:, h]
                continue
            out[kind, :, slot, :, slot], out[kind, :, slot, :, im] = ir, -ii
            out[kind, :, im, :, im], out[kind, :, im, :, slot] = ir, ii
    return out.reshape(2, 256, 256)


def inverse_jk_table(ir, ii):
    real = np.einsum("jb,kc->bcjk", ir, ir) - np.einsum("jb,kc->bcjk", ii, ii)
    imag = np.einsum("jb,kc->bcjk", ir, ii) + np.einsum("jb,kc->bcjk", ii, ir)
    out = np.zeros((N, N, N, N))
    for row in range(N):
        for slot in range(8):
            b, c = column_of(row, slot)
            if slot == 0 and b == 0:
                out[:, :, row, 0], out[:, :, row, 8] = real[0, c], real[8, c]
            else:
                out[:, :, row, slot], out[:, :, row, 8 + slot] = 2 * real[b, c], -2 * imag[b, c]
    return out.reshape(256, 256)


def packing_index():
    out = np.zeros((4, 2, 256), np.int32)
    for kind in range(4):
        for row in range(N):
            for slot in range(8):
                for part in range(2):
                    b, c = column_of(row, slot)
                    if slot == 0 and b == 0:
                        b = (8 * part, 0, 8 * (1 - part), 8)[kind]
                    place = row * 16 + 8 * part + slot
                    out[kind, 0, place] = b * 16 + c
                    out[kind, 1, place] = (N - b) % N * 16 + (N - c) % N
    return out


def kind_of(a):
    return 0 if a == 0 else 1 if a < 8 else 2 if a == 8 else 3


def pack(index_ref, all_ref, mid_ref, hot_ref, k_ref):
    for kind in range(4):
        for side in range(2):
            source = lax.broadcasted_iota(jnp.int32, (256, 256), 0)
            hot = jnp.where(source == index_ref[kind, side : side + 1, :], 1.0, 0.0)
            hot_ref[kind, side * 256 : side * 256 + 256, :] = hot.astype(BF16)
    for a in range(N):
        m = (N - a) % N
        x = jnp.concatenate(
            [all_ref[:, a * 256 : a * 256 + 256], all_ref[:, m * 256 : m * 256 + 256]], axis=1
        )
        high = x.astype(BF16)
        rest = x - high.astype(F32)
        mid = rest.astype(BF16)
        low = (rest - mid.astype(F32)).astype(BF16)
        parts = jnp.concatenate([high, mid, low], axis=0)
        o = lax.dot_general(parts, hot_ref[kind_of(a)], NN, preferred_element_type=F32)
        mid_ref[a] = 0.5 * (o[0:48] + o[48:96] + o[96:144])
    lane = lax.broadcasted_iota(jnp.int32, (48, 128), 1) // 16
    for row in range(N):
        tile = slice(row // 8 * 128, row // 8 * 128 + 128)
        for half in range(2):
            total = jnp.zeros((48, 128), F32)
            for s in range(8):
                v = mid_ref[8 * half + s, :, tile]
                shift = (s - row) % 8 * 16
                v = pltpu.roll(v, shift, 1) if shift else v
                total = jnp.where(lane == s, v, total)
            k_ref[row, :, 128 * half : 128 * half + 128] = total


ORDER = (1, 2, 3, 4, 5, 6, 7, 8, 0)


def spectrum(fr, fi, load, jt_ref, kt_ref, x1_ref, x2_ref, sr_ref, s_ref):
    def rows(t, _):
        r = pl.ds(pl.multiple_of(t * 16, 16), 16)
        for half in range(2):
            x = [load(i, r, half).astype(BF16).astype(F32) for i in range(N)]
            even = [x[0]] + [x[n] + x[N - n] for n in range(1, 8)]
            odd = [None] + [x[n] - x[N - n] for n in range(1, 8)]
            lanes = slice(half * 128, half * 128 + 128)
            for place, a in enumerate(ORDER):
                re = even[0] + x[8] if a % 2 == 0 else even[0] - x[8]
                im = None
                for n in range(1, 8):
                    c, s = float(fr[a, n]), float(fi[a, n])
                    if abs(c) > 1e-6:
                        re = re + (even[n] * c if abs(c) < 1 else even[n] if c > 0 else -even[n])
                    if abs(s) > 1e-6:
                        term = odd[n] * s
                        im = term if im is None else im + term
                im = jnp.zeros_like(re) if im is None else im
                at = pl.ds(pl.multiple_of(place * CELLS + t * 16, 16), 16)
                x1_ref[at, lanes] = re.astype(BF16)
                x1_ref[at, half * 128 + 256 : half * 128 + 384] = im.astype(BF16)
        return 0

    lax.fori_loop(0, CELLS // 16, rows, 0)
    wide = 4 * CELLS
    for first, size in ((0, wide), (wide, wide), (2 * wide, CELLS)):
        part = x1_ref[first : first + size, :]
        o = lax.dot_general(jt_ref[...], part, NT, preferred_element_type=F32)
        x2_ref[:, first : first + size] = o.astype(BF16)

    def put(kind, first, size, places):
        o = lax.dot_general(
            kt_ref[kind], x2_ref[:, first : first + size], NN, preferred_element_type=F32
        )
        for t, a in enumerate(places):
            v = o[:, t * CELLS : t * CELLS + CELLS].astype(BF16)
            sr_ref[:, a * 16 : a * 16 + 16, :] = v.reshape(N, 16, CELLS)

    put(1, 0, wide, (1, 2, 3, 4))
    put(3, 0, wide, (15, 14, 13, 12))
    put(1, wide, wide, (5, 6, 7))
    put(3, wide, wide, (11, 10, 9))
    put(2, wide + 3 * CELLS, CELLS, (8,))
    put(0, 2 * wide, CELLS, (0,))
    for row in range(N):
        s_ref[row] = sr_ref[row].astype(F32).T


CHUNKS = 2
CELLS = 128 // CHUNKS
GROUP = 8


def remote(src, dst, send, recv, peer):
    return pltpu.make_async_remote_copy(
        src_ref=src,
        dst_ref=dst,
        send_sem=send,
        recv_sem=recv,
        device_id={"vel": peer},
        device_id_type=pl.DeviceIdType.MESH,
    )


def cell_rows():
    level = (2.0 * np.arange(N) - (N - 1)) / (N - 1)
    x, y, z = np.meshgrid(level, level, level, indexing="ij")
    still = np.exp(-4.5 * (x * x + y * y + z * z))
    moving = np.exp(-0.5 * ((3.0 * x - 1.0) ** 2 + 9.0 * y * y + 9.0 * z * z))
    zero = np.zeros_like(x)
    rows = [
        np.maximum(x, 0), np.minimum(x, 0), np.maximum(y, 0), np.minimum(y, 0),
        still / still.sum(), moving / moving.sum(), zero, zero,
    ]
    out = np.stack([r.reshape(GROUP, 512) for r in rows], axis=1)
    return np.asarray(out, np.float32)


def step_body(
    fr, fi, dist_ref, type_ref, index_ref, rows_hbm, first_ref, second_ref, loss_ref,
    jt_hbm, kt_hbm, ib_hbm, ia_hbm, out_ref,
    d_ref, w_ref, t_ref, e_ref, h_ref, msg_ref, in_ref, row_ref, moved_ref,
    x_ref, r_ref, all_ref, mid_ref, hot_ref, k_ref, jt_ref, kt_ref, ib_ref, ia_ref,
    x1_ref, x2_ref, sr_ref, s_ref, z_ref, g_ref,
    send_sem, recv_sem, back_send, back_recv, own_sem, load_sem,
    dist_sem, msg_send, msg_recv, edge_send, edge_recv,
):
    me = lax.axis_index("vel")
    cell = lax.axis_index("cell")
    cells = lax.axis_size("cell")
    sides = (lax.rem(cell + cells - 1, cells), lax.rem(cell + 1, cells))
    barrier = pltpu.get_barrier_semaphore()

    def greet(place, peer):
        pl.semaphore_signal(
            barrier, inc=1, device_id={"cell": place, "vel": peer},
            device_id_type=pl.DeviceIdType.MESH,
        )

    for s in range(GROUP):
        peer = lax.rem(me + s, GROUP)
        if s:
            greet(cell, peer)
        for place in sides:
            greet(place, peer)
    slabs = [
        pltpu.make_async_copy(
            dist_ref.at[pl.ds(t * 128, 128)], d_ref.at[pl.ds(t * 128, 128)], dist_sem.at[t]
        )
        for t in range(GROUP)
    ]
    loads = [
        pltpu.make_async_copy(first_ref, all_ref.at[0:16], load_sem.at[0]),
        pltpu.make_async_copy(second_ref, all_ref.at[16:32], load_sem.at[1]),
    ]
    tables = [
        pltpu.make_async_copy(jt_hbm, jt_ref, load_sem.at[3]),
        pltpu.make_async_copy(kt_hbm, kt_ref, load_sem.at[4]),
        pltpu.make_async_copy(ib_hbm, ib_ref, load_sem.at[5]),
        pltpu.make_async_copy(ia_hbm, ia_ref, load_sem.at[6]),
    ]
    profile = pltpu.make_async_copy(rows_hbm.at[me], row_ref, load_sem.at[7])
    for copy in slabs + [profile] + loads + tables:
        copy.start()

    lane = lax.broadcasted_iota(jnp.int32, (8, 128), 1)
    total = jnp.zeros((8, 128), F32)
    for t in range(GROUP):
        slabs[t].wait()
        for u in range(16):
            x = t * 16 + u
            v = d_ref[x * 8 : x * 8 + 8, :]
            v = (v[:, :128] + v[:, 128:256]) + (v[:, 256:384] + v[:, 384:])
            total = jnp.where(lane == x, jnp.sum(v, axis=1, keepdims=True), total)
            for side in range(2):
                at = x * 8 + 7 * side
                e_ref[side, x : x + 1, :] = d_ref[at : at + 1, :]
    kinds = type_ref[...].astype(F32)
    msg_ref[0:8, :] = total
    msg_ref[8:16, :] = kinds
    in_ref[0, me] = msg_ref[...]
    pl.semaphore_wait(barrier, 3 * GROUP - 1)

    def reach(src, dst, send, recv, place, peer):
        return pltpu.make_async_remote_copy(
            src_ref=src, dst_ref=dst, send_sem=send, recv_sem=recv,
            device_id={"cell": place, "vel": peer}, device_id_type=pl.DeviceIdType.MESH,
        )

    edges = [
        reach(e_ref.at[side], h_ref.at[1 - side], edge_send.at[side], edge_recv.at[side], sides[side], me)
        for side in range(2)
    ]
    notes = []
    for s in range(GROUP):
        peer = lax.rem(me + s, GROUP)
        for kind, place in ((0, cell), (2, sides[0]), (1, sides[1])):
            if kind or s:
                notes.append(
                    reach(
                        msg_ref, in_ref.at[kind, me], msg_send.at[kind, s], msg_recv.at[kind, s],
                        place, peer,
                    )
                )
    for copy in edges + notes:
        copy.start()

    for copy in loads:
        copy.wait()
    all_ref[32:48] = jnp.broadcast_to(loss_ref[...], (16, 4096))
    pack(index_ref, all_ref, mid_ref, hot_ref, k_ref)
    profile.wait()
    for copy in notes + edges:
        copy.wait()
    still, moving = row_ref[4:5, :], row_ref[5:6, :]

    def gathered(kind):
        v = in_ref[kind]
        v = (v[0:2] + v[2:4]) + (v[4:6] + v[6:8])
        return (v[0] + v[1])[0:8]

    for side in range(2):
        density = gathered(1 + side).T[:, 7 - 7 * side : 8 - 7 * side]
        kind = in_ref[1 + side, 0, 8:16, :].T[:, 7 - 7 * side : 8 - 7 * side]
        wall = density * jnp.where(kind == 1.0, still, moving)
        inside = cell > 0 if side == 0 else cell < cells - 1
        h_ref[side] = jnp.where(kind == 0.0, h_ref[side], wall) * jnp.where(inside, 1.0, 0.0)
    density = gathered(0)
    w_ref[0:8, :] = jnp.zeros((8, 512), F32)
    w_ref[1032:1040, :] = jnp.zeros((8, 512), F32)

    def walled(t, _):
        for u in range(8):
            x = t * 8 + u
            at = pl.ds(pl.multiple_of(x * 8, 8), 8)
            here = lane == x
            kind = jnp.sum(jnp.where(here, kinds, 0.0), axis=1, keepdims=True)
            dense = jnp.sum(jnp.where(here, density, 0.0), axis=1, keepdims=True)
            wall = dense * jnp.where(kind == 1.0, still, moving)
            w = jnp.where(kind == 0.0, d_ref[at, :], wall)
            w_ref[pl.ds(pl.multiple_of(x * 8 + 8, 8), 8), :] = w
            t_ref[at, :] = jnp.broadcast_to(kind, (8, 128))
        return 0

    lax.fori_loop(0, 16, walled, 0)
    depth = lax.broadcasted_iota(jnp.int32, (8, 512), 0)

    def transport(peer, c, out_ref, *place):
        for u in range(8):
            x = peer * 16 + c * 8 + u
            low = w_ref[pl.ds(pl.multiple_of(x * 8, 8), 8), :]
            w = w_ref[pl.ds(pl.multiple_of(x * 8 + 8, 8), 8), :]
            high = w_ref[pl.ds(pl.multiple_of(x * 8 + 16, 8), 8), :]
            left = jnp.where(depth == 0, h_ref[0, pl.ds(x, 1), :], pltpu.roll(w, 1, 0))
            right = jnp.where(depth == 7, h_ref[1, pl.ds(x, 1), :], pltpu.roll(w, 7, 0))
            flow = row_ref[0:1, :] * (w - low) + row_ref[1:2, :] * (high - w)
            flow = flow + row_ref[2:3, :] * (w - left) + row_ref[3:4, :] * (right - w)
            kind = t_ref[pl.ds(pl.multiple_of(x * 8, 8), 8), :]
            kind = jnp.concatenate([kind] * 4, axis=1)
            out_ref[*place, u * 8 : u * 8 + 8, :] = jnp.where(kind == 0.0, w - courant * flow, w)

    def send(c, s):
        peer = lax.rem(me + s, GROUP)
        return remote(
            moved_ref.at[c, peer], x_ref.at[c, me], send_sem.at[c, s], recv_sem.at[c, s], peer
        )

    def first_half(s, _):
        peer = lax.rem(me + s, GROUP)
        transport(peer, 0, moved_ref, 0, peer)
        send(0, s).start()
        return 0

    def second_half(s, _):
        peer = lax.rem(me + s, GROUP)
        transport(peer, 1, moved_ref, 1, peer)
        return 0

    lax.fori_loop(1, GROUP, first_half, 0)
    lax.fori_loop(1, GROUP, second_half, 0)
    for c in range(CHUNKS):
        transport(me, c, x_ref, c, me)
    for copy in tables:
        copy.wait()
    for s in range(1, GROUP):
        send(0, s).wait_send()
    for s in range(1, GROUP):
        send(1, s).start()

    def chunk(c, _):
        for s in range(1, GROUP):
            send(c, s).wait_recv()

        def load(i, r, half):
            at = (i % 2) * 256 + half * 128
            return x_ref[c, i // 2, r, at : at + 128]

        spectrum(fr, fi, load, jt_ref, kt_ref, x1_ref, x2_ref, sr_ref, s_ref)
        g_ref[...] = jnp.zeros_like(g_ref)

        def directions(q, _):
            for row in range(N):
                s = s_ref[row]
                both = [
                    (s * k_ref[row, pl.ds(base + CHUNKS * q + t, 1), :]).astype(BF16)
                    for base in (0, 16)
                    for t in range(CHUNKS)
                ]
                kind = 1 if row % 8 == 0 else 0
                o = lax.dot_general(
                    ib_ref[kind], jnp.concatenate(both, axis=0), NT, preferred_element_type=F32
                )
                z_ref[:, row * 16 : row * 16 + 16, :] = o.astype(BF16).reshape(N, 16, 256)
            for i in range(N):
                o = lax.dot_general(ia_ref[...], z_ref[i], NN, preferred_element_type=F32)
                g_ref[i] += o[:, :128] * o[:, 128:]
            return 0

        lax.fori_loop(0, DIRS // CHUNKS, directions, 0)
        for row in range(N):
            one = (s_ref[row] * k_ref[row, 32:33, :]).astype(BF16)
            kind = 1 if row % 8 == 0 else 0
            o = lax.dot_general(ib_ref[kind], one, NT, preferred_element_type=F32)
            z_ref[:, row * 16 : row * 16 + 16, :CELLS] = o.astype(BF16).reshape(N, 16, CELLS)
        at = pl.ds(pl.multiple_of(me * 128 + c * CELLS, CELLS), CELLS)
        fluid = jnp.concatenate([t_ref[at, :]] * 2, axis=1) == 0.0

        def finish(peer):
            for h in range(2):
                i = 2 * peer + h
                loss = lax.dot_general(
                    ia_ref[...], z_ref[i, :, :CELLS], NN, preferred_element_type=F32
                )
                gain = g_ref[i].T
                gain = gain[:CELLS] + gain[CELLS:]
                x = x_ref[c, peer, :, h * 256 : h * 256 + 256]
                change = gain - x * loss.T
                r_ref[c, peer, :, h * 256 : h * 256 + 256] = jnp.where(
                    fluid, x + collision_timestep * change, x
                )

        def one(s, _):
            peer = lax.rem(me + s, GROUP)
            finish(peer)
            back(c, s).start()
            return 0

        lax.fori_loop(1, GROUP, one, 0)
        finish(me)
        pltpu.make_async_copy(r_ref.at[c, me], out_ref.at[me, c], own_sem.at[c]).start()
        return 0

    def back(c, s):
        peer = lax.rem(me + s, GROUP)
        return remote(
            r_ref.at[c, peer], out_ref.at[me, c], back_send.at[c, s], back_recv.at[c, s], peer
        )

    lax.fori_loop(0, CHUNKS, chunk, 0)
    for c in range(CHUNKS):
        pltpu.make_async_copy(r_ref.at[c, me], out_ref.at[me, c], own_sem.at[c]).wait()
        for s in range(1, GROUP):
            if c:
                send(c, s).wait_send()
            back(c, s).wait()


def constant_tables():
    fr, fi, ir, ii = line_tables()
    to = lambda t: np.asarray(t, np.float32).astype(BF16)
    tables = (j_table(fr, fi), k_tables(fr, fi), inverse_i_tables(ir, ii), inverse_jk_table(ir, ii))
    return (fr, fi), tuple(to(t) for t in tables), packing_index()


def step(distribution, cell_type, index, profiles, first, second, loss, lines, tables):
    hbm = pl.BlockSpec(memory_space=pl.ANY)
    vmem = pl.BlockSpec(memory_space=pltpu.VMEM)
    dma = pltpu.SemaphoreType.DMA
    return pl.pallas_call(
        functools.partial(step_body, *lines),
        out_shape=jax.ShapeDtypeStruct((GROUP, CHUNKS, CELLS, 512), F32),
        in_specs=[hbm, vmem, vmem] + [hbm] * 3 + [vmem] + [hbm] * 4,
        out_specs=hbm,
        scratch_shapes=[
            pltpu.VMEM((1024, 512), F32),
            pltpu.VMEM((1040, 512), F32),
            pltpu.VMEM((1024, 128), F32),
            pltpu.VMEM((2, 128, 512), F32),
            pltpu.VMEM((2, 128, 512), F32),
            pltpu.VMEM((16, 128), F32),
            pltpu.VMEM((3, GROUP, 16, 128), F32),
            pltpu.VMEM((8, 512), F32),
            pltpu.VMEM((CHUNKS, GROUP, CELLS, 512), F32),
            pltpu.VMEM((CHUNKS, GROUP, CELLS, 512), F32),
            pltpu.VMEM((CHUNKS, GROUP, CELLS, 512), F32),
            pltpu.VMEM((48, 4096), F32),
            pltpu.VMEM((N, 48, 256), F32),
            pltpu.VMEM((4, 512, 256), BF16),
            pltpu.VMEM((N, 48, 256), F32),
            pltpu.VMEM((512, 512), BF16),
            pltpu.VMEM((4, 256, 512), BF16),
            pltpu.VMEM((2, 256, 256), BF16),
            pltpu.VMEM((256, 256), BF16),
            pltpu.VMEM((9 * CELLS, 512), BF16),
            pltpu.VMEM((512, 9 * CELLS), BF16),
            pltpu.VMEM((N, 256, CELLS), BF16),
            pltpu.VMEM((N, CELLS, 256), F32),
            pltpu.VMEM((N, 256, 256), BF16),
            pltpu.VMEM((N, 256, 128), F32),
            dma((CHUNKS, GROUP)),
            dma((CHUNKS, GROUP)),
            dma((CHUNKS, GROUP)),
            dma((CHUNKS, GROUP)),
            dma((CHUNKS,)),
            dma((8,)),
            dma((GROUP,)),
            dma((3, GROUP)),
            dma((3, GROUP)),
            dma((2,)),
            dma((2,)),
        ],
        compiler_params=pltpu.CompilerParams(
            vmem_limit_bytes=62 << 20, collective_id=0, has_side_effects=True
        ),
        name="step",
    )(distribution, cell_type, index, profiles, first, second, loss, *tables)


def on_device(lines, tables, index, profiles, distribution, cell_type, first, second, loss):
    done = step(
        distribution.reshape(1024, 512),
        cell_type.T,
        index,
        profiles,
        first,
        second,
        loss.reshape(1, 4096),
        lines,
        tables,
    )
    return done.reshape(distribution.shape)


def solution(mesh):
    lines, tables, index = constant_tables()

    def body(*arguments):
        return on_device(lines, tables, index, cell_rows(), *arguments)

    return jax.shard_map(
        body,
        mesh=mesh,
        in_specs=(P(None, "cell", "vel"), P(None, "cell"), P(), P(), P()),
        out_specs=P(None, "cell", "vel"),
        check_vma=False,
    )
```

```python
import functools

import jax
import jax.numpy as jnp
import numpy as np
from jax import lax
from jax.experimental import pallas as pl
from jax.experimental.pallas import tpu as pltpu
from jax.sharding import PartitionSpec as P

N = 16
DIRS = 16
courant = 0.45
collision_timestep = 0.1
NN = (((1,), (0,)), ((), ()))
NT = (((1,), (1,)), ((), ()))
F32 = jnp.float32
BF16 = jnp.bfloat16


def bf16_values(values):
    return np.asarray(values, np.float32).astype(BF16).astype(np.float64)


def line_tables():
    n = np.arange(N)
    angle = 2 * np.pi * (n[:, None] * n[None, :] % N) / N
    c, s = np.cos(angle), np.sin(angle)
    return bf16_values(c), bf16_values(-s), bf16_values(c / N), bf16_values(s / N)


def column_of(row, slot):
    if slot == 0:
        return row % 8, 0 if row < 8 else 8
    return row, slot


def j_table(fr, fi):
    eye = np.eye(N)
    real, imag = np.kron(fr, eye), np.kron(fi, eye)
    return np.block([[real, -imag], [imag, real]])


def k_tables(fr, fi):
    out = np.zeros((4, N, N, 2, N, N))
    for kind in range(4):
        for row in range(N):
            for slot in range(8):
                b, c = column_of(row, slot)
                if slot == 0 and b == 0 and kind in (0, 2):
                    first = 0 if kind == 0 else 8
                    out[kind, row, 0, 0, first] = fr[c]
                    out[kind, row, 8, 0, 8 - first] = fr[c]
                    continue
                if slot == 0 and b == 0 and kind == 3:
                    b = 8
                if kind < 3:
                    out[kind, row, slot, 0, b], out[kind, row, slot, 1, b] = fr[c], -fi[c]
                    out[kind, row, 8 + slot, 0, b], out[kind, row, 8 + slot, 1, b] = fi[c], fr[c]
                else:
                    m = (N - b) % N
                    out[kind, row, slot, 0, m], out[kind, row, slot, 1, m] = fr[c], fi[c]
                    out[kind, row, 8 + slot, 0, m], out[kind, row, 8 + slot, 1, m] = fi[c], -fr[c]
    return out.reshape(4, 256, 512)


def inverse_i_tables(ir, ii):
    out = np.zeros((2, N, N, N, N))
    for kind in range(2):
        for slot in range(8):
            im = 8 + slot
            if kind == 1 and slot == 0:
                out[1, :, 0, 0, 0], out[1, :, 0, 8, 8] = ir[:, 0], ir[:, 8]
                out[1, :, 8, 0, 8], out[1, :, 8, 8, 0] = ir[:, 0], ir[:, 8]
                for a in range(1, 8):
                    out[1, :, 0, a, 0], out[1, :, 0, a, 8] = 2 * ir[:, a], -2 * ii[:, a]
                    h = 8 + a
                    out[1, :, 8, h, 0], out[1, :, 8, h, 8] = 2 * ir[:, h], -2 * ii[:, h]
                continue
            out[kind, :, slot, :, slot], out[kind, :, slot, :, im] = ir, -ii
            out[kind, :, im, :, im], out[kind, :, im, :, slot] = ir, ii
    return out.reshape(2, 256, 256)


def inverse_jk_table(ir, ii):
    real = np.einsum("jb,kc->bcjk", ir, ir) - np.einsum("jb,kc->bcjk", ii, ii)
    imag = np.einsum("jb,kc->bcjk", ir, ii) + np.einsum("jb,kc->bcjk", ii, ir)
    out = np.zeros((N, N, N, N))
    for row in range(N):
        for slot in range(8):
            b, c = column_of(row, slot)
            if slot == 0 and b == 0:
                out[:, :, row, 0], out[:, :, row, 8] = real[0, c], real[8, c]
            else:
                out[:, :, row, slot], out[:, :, row, 8 + slot] = 2 * real[b, c], -2 * imag[b, c]
    return out.reshape(256, 256)


def packing_index():
    out = np.zeros((4, 2, 256), np.int32)
    for kind in range(4):
        for row in range(N):
            for slot in range(8):
                for part in range(2):
                    b, c = column_of(row, slot)
                    if slot == 0 and b == 0:
                        b = (8 * part, 0, 8 * (1 - part), 8)[kind]
                    place = row * 16 + 8 * part + slot
                    out[kind, 0, place] = b * 16 + c
                    out[kind, 1, place] = (N - b) % N * 16 + (N - c) % N
    return out


def kind_of(a):
    return 0 if a == 0 else 1 if a < 8 else 2 if a == 8 else 3


def pack(index_ref, all_ref, mid_ref, hot_ref, k_ref):
    for kind in range(4):
        for side in range(2):
            source = lax.broadcasted_iota(jnp.int32, (256, 256), 0)
            hot = jnp.where(source == index_ref[kind, side : side + 1, :], 1.0, 0.0)
            hot_ref[kind, side * 256 : side * 256 + 256, :] = hot.astype(BF16)
    for a in range(N):
        m = (N - a) % N
        x = jnp.concatenate(
            [all_ref[:, a * 256 : a * 256 + 256], all_ref[:, m * 256 : m * 256 + 256]], axis=1
        )
        high = x.astype(BF16)
        rest = x - high.astype(F32)
        mid = rest.astype(BF16)
        low = (rest - mid.astype(F32)).astype(BF16)
        parts = jnp.concatenate([high, mid, low], axis=0)
        o = lax.dot_general(parts, hot_ref[kind_of(a)], NN, preferred_element_type=F32)
        mid_ref[a] = 0.5 * (o[0:48] + o[48:96] + o[96:144])
    lane = lax.broadcasted_iota(jnp.int32, (48, 128), 1) // 16
    for row in range(N):
        tile = slice(row // 8 * 128, row // 8 * 128 + 128)
        for half in range(2):
            total = jnp.zeros((48, 128), F32)
            for s in range(8):
                v = mid_ref[8 * half + s, :, tile]
                shift = (s - row) % 8 * 16
                v = pltpu.roll(v, shift, 1) if shift else v
                total = jnp.where(lane == s, v, total)
            k_ref[row, :, 128 * half : 128 * half + 128] = total


ORDER = (1, 2, 3, 4, 5, 6, 7, 8, 0)


def spectrum(fr, fi, load, jt_ref, kt_ref, x1_ref, x2_ref, sr_ref, s_ref):
    def rows(t, _):
        r = pl.ds(pl.multiple_of(t * 16, 16), 16)
        for half in range(2):
            x = [load(i, r, half).astype(BF16).astype(F32) for i in range(N)]
            even = [x[0]] + [x[n] + x[N - n] for n in range(1, 8)]
            odd = [None] + [x[n] - x[N - n] for n in range(1, 8)]
            lanes = slice(half * 128, half * 128 + 128)
            for place, a in enumerate(ORDER):
                re = even[0] + x[8] if a % 2 == 0 else even[0] - x[8]
                im = None
                for n in range(1, 8):
                    c, s = float(fr[a, n]), float(fi[a, n])
                    if abs(c) > 1e-6:
                        re = re + (even[n] * c if abs(c) < 1 else even[n] if c > 0 else -even[n])
                    if abs(s) > 1e-6:
                        term = odd[n] * s
                        im = term if im is None else im + term
                im = jnp.zeros_like(re) if im is None else im
                at = pl.ds(pl.multiple_of(place * CELLS + t * 16, 16), 16)
                x1_ref[at, lanes] = re.astype(BF16)
                x1_ref[at, half * 128 + 256 : half * 128 + 384] = im.astype(BF16)
        return 0

    lax.fori_loop(0, CELLS // 16, rows, 0)
    wide = 8 * CELLS
    for first, size in ((0, wide), (wide, CELLS)):
        part = x1_ref[first : first + size, :]
        o = lax.dot_general(jt_ref[...], part, NT, preferred_element_type=F32)
        x2_ref[:, first : first + size] = o.astype(BF16)

    def put(kind, first, size, places):
        o = lax.dot_general(
            kt_ref[kind], x2_ref[:, first : first + size], NN, preferred_element_type=F32
        )
        for t, a in enumerate(places):
            v = o[:, t * CELLS : t * CELLS + CELLS].astype(BF16).reshape(N, 16, CELLS)
            for row in range(N):
                at = row % CHUNKS * CELLS
                sr_ref[row // CHUNKS, a * 16 : a * 16 + 16, at : at + CELLS] = v[row]

    put(1, 0, wide, (1, 2, 3, 4, 5, 6, 7))
    put(3, 0, wide, (15, 14, 13, 12, 11, 10, 9))
    put(2, 7 * CELLS, CELLS, (8,))
    put(0, wide, CELLS, (0,))
    for t in range(N // CHUNKS):
        s_ref[CHUNKS * t : CHUNKS * t + CHUNKS] = sr_ref[t].astype(F32).T.reshape(CHUNKS, CELLS, 256)


CHUNKS = 4
CELLS = 128 // CHUNKS
ROWS = CELLS // 8
NEED = [
    [15] * (c == 0) + [u for u in range(c * ROWS + (c > 0), c * ROWS + ROWS + 1) if u < 15]
    for c in range(CHUNKS)
]
GROUP = 8


def remote(src, dst, send, recv, peer):
    return pltpu.make_async_remote_copy(
        src_ref=src,
        dst_ref=dst,
        send_sem=send,
        recv_sem=recv,
        device_id={"vel": peer},
        device_id_type=pl.DeviceIdType.MESH,
    )


def cell_rows():
    level = (2.0 * np.arange(N) - (N - 1)) / (N - 1)
    x, y, z = np.meshgrid(level, level, level, indexing="ij")
    still = np.exp(-4.5 * (x * x + y * y + z * z))
    moving = np.exp(-0.5 * ((3.0 * x - 1.0) ** 2 + 9.0 * y * y + 9.0 * z * z))
    zero = np.zeros_like(x)
    rows = [
        np.maximum(x, 0), np.minimum(x, 0), np.maximum(y, 0), np.minimum(y, 0),
        still / still.sum(), moving / moving.sum(), zero, zero,
    ]
    out = np.stack([r.reshape(GROUP, 512) for r in rows], axis=1)
    return np.asarray(out, np.float32)


def step_body(
    fr, fi, dist_ref, type_ref, index_ref, rows_hbm, first_ref, second_ref, loss_ref,
    jt_hbm, kt_hbm, ib_hbm, ia_hbm, out_ref,
    d_ref, w_ref, t_ref, e_ref, h_ref, side_ref, msg_ref, in_ref, row_ref, moved_ref,
    x_ref, r_ref, all_ref, mid_ref, hot_ref, k_ref, jt_ref, kt_ref, ib_ref, ia_ref,
    x1_ref, x2_ref, sr_ref, s_ref, zl_ref, l_ref, z_ref, g_ref,
    send_sem, recv_sem, back_send, back_recv, own_sem, load_sem,
    dist_sem, msg_send, msg_recv, edge_send, edge_recv,
):
    me = lax.axis_index("vel")
    cell = lax.axis_index("cell")
    cells = lax.axis_size("cell")
    sides = (lax.rem(cell + cells - 1, cells), lax.rem(cell + 1, cells))
    barrier = pltpu.get_barrier_semaphore()

    def greet(place, peer):
        pl.semaphore_signal(
            barrier, inc=1, device_id={"cell": place, "vel": peer},
            device_id_type=pl.DeviceIdType.MESH,
        )

    for s in range(GROUP):
        peer = lax.rem(me + s, GROUP)
        if s:
            greet(cell, peer)
        for place in sides:
            greet(place, peer)
    slabs = [
        pltpu.make_async_copy(
            dist_ref.at[pl.ds(t * 128, 128)], d_ref.at[pl.ds(t * 128, 128)], dist_sem.at[t]
        )
        for t in range(GROUP)
    ]
    loads = [
        pltpu.make_async_copy(first_ref, all_ref.at[0:16], load_sem.at[0]),
        pltpu.make_async_copy(second_ref, all_ref.at[16:32], load_sem.at[1]),
    ]
    tables = [
        pltpu.make_async_copy(jt_hbm, jt_ref, load_sem.at[3]),
        pltpu.make_async_copy(kt_hbm, kt_ref, load_sem.at[4]),
        pltpu.make_async_copy(ib_hbm, ib_ref, load_sem.at[5]),
        pltpu.make_async_copy(ia_hbm, ia_ref, load_sem.at[6]),
    ]
    profile = pltpu.make_async_copy(rows_hbm.at[me], row_ref, load_sem.at[7])
    for copy in slabs + [profile] + loads + tables:
        copy.start()

    lane = lax.broadcasted_iota(jnp.int32, (8, 128), 1)
    total = jnp.zeros((8, 128), F32)
    for t in range(GROUP):
        slabs[t].wait()
        for u in range(16):
            x = t * 16 + u
            v = d_ref[x * 8 : x * 8 + 8, :]
            v = (v[:, :128] + v[:, 128:256]) + (v[:, 256:384] + v[:, 384:])
            total = jnp.where(lane == x, jnp.sum(v, axis=1, keepdims=True), total)
            for side in range(2):
                at = x * 8 + 7 * side
                place = t * ROWS + u % ROWS
                e_ref[side, u // ROWS, place : place + 1, :] = d_ref[at : at + 1, :]
    kinds = type_ref[...].astype(F32)
    msg_ref[0:8, :] = total
    msg_ref[8:16, :] = kinds
    in_ref[0, me] = msg_ref[...]
    pl.semaphore_wait(barrier, 3 * GROUP - 1)

    def reach(src, dst, send, recv, place, peer):
        return pltpu.make_async_remote_copy(
            src_ref=src, dst_ref=dst, send_sem=send, recv_sem=recv,
            device_id={"cell": place, "vel": peer}, device_id_type=pl.DeviceIdType.MESH,
        )

    edges = [
        reach(
            e_ref.at[side, c], h_ref.at[1 - side, c], edge_send.at[side, c], edge_recv.at[side, c],
            sides[side], me,
        )
        for c in range(CHUNKS)
        for side in range(2)
    ]
    notes = []
    for s in range(GROUP):
        peer = lax.rem(me + s, GROUP)
        for kind, place in ((0, cell), (2, sides[0]), (1, sides[1])):
            if kind or s:
                notes.append(
                    reach(
                        msg_ref, in_ref.at[kind, me], msg_send.at[kind, s], msg_recv.at[kind, s],
                        place, peer,
                    )
                )
    for copy in edges[:2] + notes + edges[2:]:
        copy.start()

    def types(t, _):
        for u in range(8):
            x = t * 8 + u
            kind = jnp.sum(jnp.where(lane == x, kinds, 0.0), axis=1, keepdims=True)
            t_ref[pl.ds(pl.multiple_of(x * 8, 8), 8), :] = jnp.broadcast_to(kind, (8, 128))
        return 0

    lax.fori_loop(0, 16, types, 0)

    for copy in loads:
        copy.wait()
    all_ref[32:48] = jnp.broadcast_to(loss_ref[...], (16, 4096))
    pack(index_ref, all_ref, mid_ref, hot_ref, k_ref)
    profile.wait()
    for copy in notes:
        copy.wait()
    still, moving = row_ref[4:5, :], row_ref[5:6, :]

    def gathered(kind):
        v = in_ref[kind]
        v = (v[0:2] + v[2:4]) + (v[4:6] + v[6:8])
        return (v[0] + v[1])[0:8]

    for side in range(2):
        edge = slice(7 - 7 * side, 8 - 7 * side)
        sums = jnp.broadcast_to(gathered(1 + side)[edge], (8, 128))
        side_ref[side, 0] = sums.T
        side_ref[side, 1] = jnp.broadcast_to(in_ref[1 + side, 0, 8:16, :][edge], (8, 128)).T

    def halo(c):
        for side in range(2):
            edges[2 * c + side].wait()
        for side in range(2):
            column = [
                jnp.concatenate(
                    [side_ref[side, k, d * 16 + c * ROWS : d * 16 + c * ROWS + ROWS, :] for d in range(GROUP)],
                    axis=0,
                )[:, 0:1]
                for k in range(2)
            ]
            wall = column[0] * jnp.where(column[1] == 1.0, still, moving)
            inside = cell > 0 if side == 0 else cell < cells - 1
            raw = h_ref[side, c]
            h_ref[side, c] = jnp.where(column[1] == 0.0, raw, wall) * jnp.where(inside, 1.0, 0.0)

    density = gathered(0)
    w_ref[0:8, :] = jnp.zeros((8, 512), F32)
    w_ref[1032:1040, :] = jnp.zeros((8, 512), F32)

    def walled(rows):
        def body(t, _):
            for u in rows:
                x = t * 16 + u
                at = pl.ds(pl.multiple_of(x * 8, 8), 8)
                kind = jnp.concatenate([t_ref[at, :]] * 4, axis=1)
                dense = jnp.sum(jnp.where(lane == x, density, 0.0), axis=1, keepdims=True)
                wall = dense * jnp.where(kind == 1.0, still, moving)
                w = jnp.where(kind == 0.0, d_ref[at, :], wall)
                w_ref[pl.ds(pl.multiple_of(x * 8 + 8, 8), 8), :] = w
            return 0

        lax.fori_loop(0, GROUP, body, 0)

    depth = lax.broadcasted_iota(jnp.int32, (8, 512), 0)

    def transport(peer, c, out_ref, *place):
        for u in range(ROWS):
            x = peer * 16 + c * ROWS + u
            low = w_ref[pl.ds(pl.multiple_of(x * 8, 8), 8), :]
            w = w_ref[pl.ds(pl.multiple_of(x * 8 + 8, 8), 8), :]
            high = w_ref[pl.ds(pl.multiple_of(x * 8 + 16, 8), 8), :]
            left = jnp.where(depth == 0, h_ref[0, c, pl.ds(peer * ROWS + u, 1), :], pltpu.roll(w, 1, 0))
            right = jnp.where(depth == 7, h_ref[1, c, pl.ds(peer * ROWS + u, 1), :], pltpu.roll(w, 7, 0))
            flow = row_ref[0:1, :] * (w - low) + row_ref[1:2, :] * (high - w)
            flow = flow + row_ref[2:3, :] * (w - left) + row_ref[3:4, :] * (right - w)
            kind = t_ref[pl.ds(pl.multiple_of(x * 8, 8), 8), :]
            kind = jnp.concatenate([kind] * 4, axis=1)
            out_ref[*place, u * 8 : u * 8 + 8, :] = jnp.where(kind == 0.0, w - courant * flow, w)

    def send(c, s):
        peer = lax.rem(me + s, GROUP)
        return remote(
            moved_ref.at[c, peer], x_ref.at[c, me], send_sem.at[c, s], recv_sem.at[c, s], peer
        )

    for c in range(CHUNKS):
        walled(NEED[c])
        halo(c)

        def part(s, _):
            peer = lax.rem(me + s, GROUP)
            transport(peer, c, moved_ref, c, peer)
            send(c, s).start()
            return 0

        lax.fori_loop(1, GROUP, part, 0)
        transport(me, c, x_ref, c, me)
    for copy in tables:
        copy.wait()

    def chunk(c, _):
        for s in range(1, GROUP):
            send(c, s).wait_recv()

        def load(i, r, half):
            at = (i % 2) * 256 + half * 128
            return x_ref[c, i // 2, r, at : at + 128]

        spectrum(fr, fi, load, jt_ref, kt_ref, x1_ref, x2_ref, sr_ref, s_ref)
        g_ref[...] = jnp.zeros_like(g_ref)

        def directions(q, _):
            for row in range(N):
                s = s_ref[row]
                both = [
                    (s * k_ref[row, pl.ds(base + CHUNKS * q + t, 1), :]).astype(BF16)
                    for base in (0, 16)
                    for t in range(CHUNKS)
                ]
                kind = 1 if row % 8 == 0 else 0
                o = lax.dot_general(
                    ib_ref[kind], jnp.concatenate(both, axis=0), NT, preferred_element_type=F32
                )
                z_ref[:, row * 16 : row * 16 + 16, :] = o.astype(BF16).reshape(N, 16, 256)
            for i in range(N):
                o = lax.dot_general(ia_ref[...], z_ref[i], NN, preferred_element_type=F32)
                g_ref[i] += o[:, :128] * o[:, 128:]
            return 0

        lax.fori_loop(0, DIRS // CHUNKS, directions, 0)
        for row in range(N):
            one = (s_ref[row] * k_ref[row, 32:33, :]).astype(BF16)
            kind = 1 if row % 8 == 0 else 0
            o = lax.dot_general(
                ib_ref[kind], jnp.concatenate([one] * CHUNKS, axis=0), NT, preferred_element_type=F32
            ).astype(BF16)
            for i in range(N):
                lanes = slice(i % CHUNKS * CELLS, i % CHUNKS * CELLS + CELLS)
                zl_ref[i // CHUNKS, row * 16 : row * 16 + 16, lanes] = o[i * 16 : i * 16 + 16, lanes]
        for t in range(N // CHUNKS):
            o = lax.dot_general(ia_ref[...], zl_ref[t], NN, preferred_element_type=F32)
            l_ref[CHUNKS * t : CHUNKS * t + CHUNKS] = o.T.reshape(CHUNKS, CELLS, 256)
        at = pl.ds(pl.multiple_of(me * 128 + c * CELLS, CELLS), CELLS)
        fluid = jnp.concatenate([t_ref[at, :]] * 2, axis=1) == 0.0

        def finish(peer):
            for h in range(2):
                i = 2 * peer + h
                gain = g_ref[i].T
                gain = sum(gain[t * CELLS : t * CELLS + CELLS] for t in range(CHUNKS))
                x = x_ref[c, peer, :, h * 256 : h * 256 + 256]
                change = gain - x * l_ref[i]
                r_ref[c, peer, :, h * 256 : h * 256 + 256] = jnp.where(
                    fluid, x + collision_timestep * change, x
                )

        for group in ((1, 2, 3), (4, 5, 6, 7)):
            for s in group:
                finish(lax.rem(me + s, GROUP))
            for s in group:
                back(c, s).start()
        finish(me)
        pltpu.make_async_copy(r_ref.at[c, me], out_ref.at[me, c], own_sem.at[c]).start()
        return 0

    def back(c, s):
        peer = lax.rem(me + s, GROUP)
        return remote(
            r_ref.at[c, peer], out_ref.at[me, c], back_send.at[c, s], back_recv.at[c, s], peer
        )

    lax.fori_loop(0, CHUNKS, chunk, 0)
    for c in range(CHUNKS):
        pltpu.make_async_copy(r_ref.at[c, me], out_ref.at[me, c], own_sem.at[c]).wait()
        for s in range(1, GROUP):
            send(c, s).wait_send()
            back(c, s).wait()


def constant_tables():
    fr, fi, ir, ii = line_tables()
    to = lambda t: np.asarray(t, np.float32).astype(BF16)
    tables = (j_table(fr, fi), k_tables(fr, fi), inverse_i_tables(ir, ii), inverse_jk_table(ir, ii))
    return (fr, fi), tuple(to(t) for t in tables), packing_index()


def step(distribution, cell_type, index, profiles, first, second, loss, lines, tables):
    hbm = pl.BlockSpec(memory_space=pl.ANY)
    vmem = pl.BlockSpec(memory_space=pltpu.VMEM)
    dma = pltpu.SemaphoreType.DMA
    return pl.pallas_call(
        functools.partial(step_body, *lines),
        out_shape=jax.ShapeDtypeStruct((GROUP, CHUNKS, CELLS, 512), F32),
        in_specs=[hbm, vmem, vmem] + [hbm] * 3 + [vmem] + [hbm] * 4,
        out_specs=vmem,
        scratch_shapes=[
            pltpu.VMEM((1024, 512), F32),
            pltpu.VMEM((1040, 512), F32),
            pltpu.VMEM((1024, 128), F32),
            pltpu.VMEM((2, CHUNKS, 8 * ROWS, 512), F32),
            pltpu.VMEM((2, CHUNKS, 8 * ROWS, 512), F32),
            pltpu.VMEM((2, 2, 128, 8), F32),
            pltpu.VMEM((16, 128), F32),
            pltpu.VMEM((3, GROUP, 16, 128), F32),
            pltpu.VMEM((8, 512), F32),
            pltpu.VMEM((CHUNKS, GROUP, CELLS, 512), F32),
            pltpu.VMEM((CHUNKS, GROUP, CELLS, 512), F32),
            pltpu.VMEM((CHUNKS, GROUP, CELLS, 512), F32),
            pltpu.VMEM((48, 4096), F32),
            pltpu.VMEM((N, 48, 256), F32),
            pltpu.VMEM((4, 512, 256), BF16),
            pltpu.VMEM((N, 48, 256), F32),
            pltpu.VMEM((512, 512), BF16),
            pltpu.VMEM((4, 256, 512), BF16),
            pltpu.VMEM((2, 256, 256), BF16),
            pltpu.VMEM((256, 256), BF16),
            pltpu.VMEM((9 * CELLS, 512), BF16),
            pltpu.VMEM((512, 9 * CELLS), BF16),
            pltpu.VMEM((N // CHUNKS, 256, 128), BF16),
            pltpu.VMEM((N, CELLS, 256), F32),
            pltpu.VMEM((N // CHUNKS, 256, 128), BF16),
            pltpu.VMEM((N, CELLS, 256), F32),
            pltpu.VMEM((N, 256, 256), BF16),
            pltpu.VMEM((N, 256, 128), F32),
            dma((CHUNKS, GROUP)),
            dma((CHUNKS, GROUP)),
            dma((CHUNKS, GROUP)),
            dma((CHUNKS, GROUP)),
            dma((CHUNKS,)),
            dma((8,)),
            dma((GROUP,)),
            dma((3, GROUP)),
            dma((3, GROUP)),
            dma((2, CHUNKS)),
            dma((2, CHUNKS)),
        ],
        compiler_params=pltpu.CompilerParams(
            vmem_limit_bytes=62 << 20, collective_id=0, has_side_effects=True
        ),
        name="step",
    )(distribution, cell_type, index, profiles, first, second, loss, *tables)


def on_device(lines, tables, index, profiles, distribution, cell_type, first, second, loss):
    done = step(
        distribution.reshape(1024, 512),
        cell_type.T,
        index,
        profiles,
        first,
        second,
        loss.reshape(1, 4096),
        lines,
        tables,
    )
    return done.reshape(distribution.shape)


def solution(mesh):
    lines, tables, index = constant_tables()

    def body(*arguments):
        return on_device(lines, tables, index, cell_rows(), *arguments)

    return jax.shard_map(
        body,
        mesh=mesh,
        in_specs=(P(None, "cell", "vel"), P(None, "cell"), P(), P(), P()),
        out_specs=P(None, "cell", "vel"),
        check_vma=False,
    )
```

```python
import functools

import jax
import jax.numpy as jnp
import numpy as np
from jax import lax
from jax.experimental import pallas as pl
from jax.experimental.pallas import tpu as pltpu
from jax.sharding import PartitionSpec as P

N = 16
DIRS = 16
courant = 0.45
collision_timestep = 0.1
NN = (((1,), (0,)), ((), ()))
NT = (((1,), (1,)), ((), ()))
F32 = jnp.float32
BF16 = jnp.bfloat16


def bf16_values(values):
    return np.asarray(values, np.float32).astype(BF16).astype(np.float64)


def line_tables():
    n = np.arange(N)
    angle = 2 * np.pi * (n[:, None] * n[None, :] % N) / N
    c, s = np.cos(angle), np.sin(angle)
    return bf16_values(c), bf16_values(-s), bf16_values(c / N), bf16_values(s / N)


def column_of(row, slot):
    if slot == 0:
        return row % 8, 0 if row < 8 else 8
    return row, slot


def j_table(fr, fi):
    eye = np.eye(N)
    real, imag = np.kron(fr, eye), np.kron(fi, eye)
    return np.block([[real, -imag], [imag, real]])


def k_tables(fr, fi):
    out = np.zeros((4, N, N, 2, N, N))
    for kind in range(4):
        for row in range(N):
            for slot in range(8):
                b, c = column_of(row, slot)
                if slot == 0 and b == 0 and kind in (0, 2):
                    first = 0 if kind == 0 else 8
                    out[kind, row, 0, 0, first] = fr[c]
                    out[kind, row, 8, 0, 8 - first] = fr[c]
                    continue
                if slot == 0 and b == 0 and kind == 3:
                    b = 8
                if kind < 3:
                    out[kind, row, slot, 0, b], out[kind, row, slot, 1, b] = fr[c], -fi[c]
                    out[kind, row, 8 + slot, 0, b], out[kind, row, 8 + slot, 1, b] = fi[c], fr[c]
                else:
                    m = (N - b) % N
                    out[kind, row, slot, 0, m], out[kind, row, slot, 1, m] = fr[c], fi[c]
                    out[kind, row, 8 + slot, 0, m], out[kind, row, 8 + slot, 1, m] = fi[c], -fr[c]
    return out.reshape(4, 256, 512)


def inverse_i_tables(ir, ii):
    out = np.zeros((2, N, N, N, N))
    for kind in range(2):
        for slot in range(8):
            im = 8 + slot
            if kind == 1 and slot == 0:
                out[1, :, 0, 0, 0], out[1, :, 0, 8, 8] = ir[:, 0], ir[:, 8]
                out[1, :, 8, 0, 8], out[1, :, 8, 8, 0] = ir[:, 0], ir[:, 8]
                for a in range(1, 8):
                    out[1, :, 0, a, 0], out[1, :, 0, a, 8] = 2 * ir[:, a], -2 * ii[:, a]
                    h = 8 + a
                    out[1, :, 8, h, 0], out[1, :, 8, h, 8] = 2 * ir[:, h], -2 * ii[:, h]
                continue
            out[kind, :, slot, :, slot], out[kind, :, slot, :, im] = ir, -ii
            out[kind, :, im, :, im], out[kind, :, im, :, slot] = ir, ii
    return out.reshape(2, 256, 256)


def inverse_jk_table(ir, ii):
    real = np.einsum("jb,kc->bcjk", ir, ir) - np.einsum("jb,kc->bcjk", ii, ii)
    imag = np.einsum("jb,kc->bcjk", ir, ii) + np.einsum("jb,kc->bcjk", ii, ir)
    out = np.zeros((N, N, N, N))
    for row in range(N):
        for slot in range(8):
            b, c = column_of(row, slot)
            if slot == 0 and b == 0:
                out[:, :, row, 0], out[:, :, row, 8] = real[0, c], real[8, c]
            else:
                out[:, :, row, slot], out[:, :, row, 8 + slot] = 2 * real[b, c], -2 * imag[b, c]
    return out.reshape(256, 256)


def packing_index():
    out = np.zeros((4, 2, 256), np.int32)
    for kind in range(4):
        for row in range(N):
            for slot in range(8):
                for part in range(2):
                    b, c = column_of(row, slot)
                    if slot == 0 and b == 0:
                        b = (8 * part, 0, 8 * (1 - part), 8)[kind]
                    place = row * 16 + 8 * part + slot
                    out[kind, 0, place] = b * 16 + c
                    out[kind, 1, place] = (N - b) % N * 16 + (N - c) % N
    return out


def kind_of(a):
    return 0 if a == 0 else 1 if a < 8 else 2 if a == 8 else 3


def pack(index_ref, all_ref, mid_ref, hot_ref, k_ref):
    for kind in range(4):
        for side in range(2):
            source = lax.broadcasted_iota(jnp.int32, (256, 256), 0)
            hot = jnp.where(source == index_ref[kind, side : side + 1, :], 1.0, 0.0)
            hot_ref[kind, side * 256 : side * 256 + 256, :] = hot.astype(BF16)
    for a in range(N):
        m = (N - a) % N
        x = jnp.concatenate(
            [all_ref[:, a * 256 : a * 256 + 256], all_ref[:, m * 256 : m * 256 + 256]], axis=1
        )
        high = x.astype(BF16)
        rest = x - high.astype(F32)
        mid = rest.astype(BF16)
        low = (rest - mid.astype(F32)).astype(BF16)
        parts = jnp.concatenate([high, mid, low], axis=0)
        o = lax.dot_general(parts, hot_ref[kind_of(a)], NN, preferred_element_type=F32)
        mid_ref[a] = 0.5 * (o[0:48] + o[48:96] + o[96:144])
    lane = lax.broadcasted_iota(jnp.int32, (48, 128), 1) // 16
    for row in range(N):
        tile = slice(row // 8 * 128, row // 8 * 128 + 128)
        for half in range(2):
            total = jnp.zeros((48, 128), F32)
            for s in range(8):
                v = mid_ref[8 * half + s, :, tile]
                shift = (s - row) % 8 * 16
                v = pltpu.roll(v, shift, 1) if shift else v
                total = jnp.where(lane == s, v, total)
            k_ref[row, :, 128 * half : 128 * half + 128] = total


ORDER = (1, 2, 3, 4, 5, 6, 7, 8, 0)


def spectrum(fr, fi, load, jt_ref, kt_ref, x1_ref, x2_ref, sr_ref, s_ref):
    def rows(t, _):
        r = pl.ds(pl.multiple_of(t * 16, 16), 16)
        for half in range(2):
            x = [load(i, r, half).astype(BF16).astype(F32) for i in range(N)]
            even = [x[0]] + [x[n] + x[N - n] for n in range(1, 8)]
            odd = [None] + [x[n] - x[N - n] for n in range(1, 8)]
            lanes = slice(half * 128, half * 128 + 128)
            for place, a in enumerate(ORDER):
                re = even[0] + x[8] if a % 2 == 0 else even[0] - x[8]
                im = None
                for n in range(1, 8):
                    c, s = float(fr[a, n]), float(fi[a, n])
                    if abs(c) > 1e-6:
                        re = re + (even[n] * c if abs(c) < 1 else even[n] if c > 0 else -even[n])
                    if abs(s) > 1e-6:
                        term = odd[n] * s
                        im = term if im is None else im + term
                im = jnp.zeros_like(re) if im is None else im
                at = pl.ds(pl.multiple_of(place * CELLS + t * 16, 16), 16)
                x1_ref[at, lanes] = re.astype(BF16)
                x1_ref[at, half * 128 + 256 : half * 128 + 384] = im.astype(BF16)
        return 0

    lax.fori_loop(0, CELLS // 16, rows, 0)
    wide = 8 * CELLS
    for first, size in ((0, wide), (wide, CELLS)):
        part = x1_ref[first : first + size, :]
        o = lax.dot_general(jt_ref[...], part, NT, preferred_element_type=F32)
        x2_ref[:, first : first + size] = o.astype(BF16)

    def put(kind, first, size, places):
        o = lax.dot_general(
            kt_ref[kind], x2_ref[:, first : first + size], NN, preferred_element_type=F32
        )
        for t, a in enumerate(places):
            v = o[:, t * CELLS : t * CELLS + CELLS].astype(BF16).reshape(N, 16, CELLS)
            for row in range(N):
                at = row % CHUNKS * CELLS
                sr_ref[row // CHUNKS, a * 16 : a * 16 + 16, at : at + CELLS] = v[row]

    put(1, 0, wide, (1, 2, 3, 4, 5, 6, 7))
    put(3, 0, wide, (15, 14, 13, 12, 11, 10, 9))
    put(2, 7 * CELLS, CELLS, (8,))
    put(0, wide, CELLS, (0,))
    for t in range(N // CHUNKS):
        s_ref[CHUNKS * t : CHUNKS * t + CHUNKS] = sr_ref[t].astype(F32).T.reshape(CHUNKS, CELLS, 256)


CHUNKS = 4
CELLS = 128 // CHUNKS
ROWS = CELLS // 8
NEED = [
    [15] * (c == 0) + [u for u in range(c * ROWS + (c > 0), c * ROWS + ROWS + 1) if u < 15]
    for c in range(CHUNKS)
]
GROUP = 8


def remote(src, dst, send, recv, peer):
    return pltpu.make_async_remote_copy(
        src_ref=src,
        dst_ref=dst,
        send_sem=send,
        recv_sem=recv,
        device_id={"vel": peer},
        device_id_type=pl.DeviceIdType.MESH,
    )


def cell_rows():
    level = (2.0 * np.arange(N) - (N - 1)) / (N - 1)
    x, y, z = np.meshgrid(level, level, level, indexing="ij")
    still = np.exp(-4.5 * (x * x + y * y + z * z))
    moving = np.exp(-0.5 * ((3.0 * x - 1.0) ** 2 + 9.0 * y * y + 9.0 * z * z))
    zero = np.zeros_like(x)
    rows = [
        np.maximum(x, 0), np.minimum(x, 0), np.maximum(y, 0), np.minimum(y, 0),
        still / still.sum(), moving / moving.sum(), zero, zero,
    ]
    out = np.stack([r.reshape(GROUP, 512) for r in rows], axis=1)
    return np.asarray(out, np.float32)


def step_body(
    fr, fi, dist_ref, type_ref, index_ref, rows_hbm, first_ref, second_ref, loss_ref,
    jt_hbm, kt_hbm, ib_hbm, ia_hbm, out_ref,
    d_ref, w_ref, t_ref, e_ref, h_ref, side_ref, msg_ref, in_ref, row_ref, moved_ref,
    x_ref, r_ref, all_ref, mid_ref, hot_ref, k_ref, jt_ref, kt_ref, ib_ref, ia_ref,
    x1_ref, x2_ref, sr_ref, s_ref, zl_ref, l_ref, z_ref, g_ref,
    send_sem, recv_sem, back_send, back_recv, own_sem, load_sem,
    dist_sem, msg_send, msg_recv, edge_send, edge_recv,
):
    me = lax.axis_index("vel")
    cell = lax.axis_index("cell")
    cells = lax.axis_size("cell")
    sides = (lax.rem(cell + cells - 1, cells), lax.rem(cell + 1, cells))
    barrier = pltpu.get_barrier_semaphore()

    def greet(place, peer):
        pl.semaphore_signal(
            barrier, inc=1, device_id={"cell": place, "vel": peer},
            device_id_type=pl.DeviceIdType.MESH,
        )

    for s in range(GROUP):
        peer = lax.rem(me + s, GROUP)
        if s:
            greet(cell, peer)
        for place in sides:
            greet(place, peer)
    slabs = [
        pltpu.make_async_copy(
            dist_ref.at[pl.ds(t * 128, 128)], d_ref.at[pl.ds(t * 128, 128)], dist_sem.at[t]
        )
        for t in range(GROUP)
    ]
    loads = [
        pltpu.make_async_copy(first_ref, all_ref.at[0:16], load_sem.at[0]),
        pltpu.make_async_copy(second_ref, all_ref.at[16:32], load_sem.at[1]),
    ]
    tables = [
        pltpu.make_async_copy(jt_hbm, jt_ref, load_sem.at[3]),
        pltpu.make_async_copy(kt_hbm, kt_ref, load_sem.at[4]),
        pltpu.make_async_copy(ib_hbm, ib_ref, load_sem.at[5]),
        pltpu.make_async_copy(ia_hbm, ia_ref, load_sem.at[6]),
    ]
    profile = pltpu.make_async_copy(rows_hbm.at[me], row_ref, load_sem.at[7])
    for copy in slabs + [profile] + loads + tables:
        copy.start()

    lane = lax.broadcasted_iota(jnp.int32, (8, 128), 1)
    total = jnp.zeros((8, 128), F32)
    for t in range(GROUP):
        slabs[t].wait()
        for u in range(16):
            x = t * 16 + u
            v = d_ref[x * 8 : x * 8 + 8, :]
            v = (v[:, :128] + v[:, 128:256]) + (v[:, 256:384] + v[:, 384:])
            total = jnp.where(lane == x, jnp.sum(v, axis=1, keepdims=True), total)
            for side in range(2):
                at = x * 8 + 7 * side
                place = t * ROWS + u % ROWS
                e_ref[side, u // ROWS, place : place + 1, :] = d_ref[at : at + 1, :]
    kinds = type_ref[...].astype(F32)
    msg_ref[0:8, :] = total
    msg_ref[8:16, :] = kinds
    in_ref[0, me] = msg_ref[...]
    pl.semaphore_wait(barrier, 3 * GROUP - 1)

    def reach(src, dst, send, recv, place, peer):
        return pltpu.make_async_remote_copy(
            src_ref=src, dst_ref=dst, send_sem=send, recv_sem=recv,
            device_id={"cell": place, "vel": peer}, device_id_type=pl.DeviceIdType.MESH,
        )

    edges = [
        reach(
            e_ref.at[side, c], h_ref.at[1 - side, c], edge_send.at[side, c], edge_recv.at[side, c],
            sides[side], me,
        )
        for c in range(CHUNKS)
        for side in range(2)
    ]
    notes = []
    for s in range(GROUP):
        peer = lax.rem(me + s, GROUP)
        for kind, place in ((0, cell), (2, sides[0]), (1, sides[1])):
            if kind or s:
                notes.append(
                    reach(
                        msg_ref, in_ref.at[kind, me], msg_send.at[kind, s], msg_recv.at[kind, s],
                        place, peer,
                    )
                )
    for copy in edges[:2] + notes + edges[2:]:
        copy.start()

    def types(t, _):
        for u in range(8):
            x = t * 8 + u
            kind = jnp.sum(jnp.where(lane == x, kinds, 0.0), axis=1, keepdims=True)
            t_ref[pl.ds(pl.multiple_of(x * 8, 8), 8), :] = jnp.broadcast_to(kind, (8, 128))
        return 0

    lax.fori_loop(0, 16, types, 0)

    for copy in loads:
        copy.wait()
    all_ref[32:48] = jnp.broadcast_to(loss_ref[...], (16, 4096))
    profile.wait()
    for copy in notes:
        copy.wait()
    still, moving = row_ref[4:5, :], row_ref[5:6, :]

    def gathered(kind):
        v = in_ref[kind]
        v = (v[0:2] + v[2:4]) + (v[4:6] + v[6:8])
        return (v[0] + v[1])[0:8]

    for side in range(2):
        edge = slice(7 - 7 * side, 8 - 7 * side)
        sums = jnp.broadcast_to(gathered(1 + side)[edge], (8, 128))
        side_ref[side, 0] = sums.T
        side_ref[side, 1] = jnp.broadcast_to(in_ref[1 + side, 0, 8:16, :][edge], (8, 128)).T

    def halo(c):
        for side in range(2):
            edges[2 * c + side].wait()
        for side in range(2):
            column = [
                jnp.concatenate(
                    [side_ref[side, k, d * 16 + c * ROWS : d * 16 + c * ROWS + ROWS, :] for d in range(GROUP)],
                    axis=0,
                )[:, 0:1]
                for k in range(2)
            ]
            wall = column[0] * jnp.where(column[1] == 1.0, still, moving)
            inside = cell > 0 if side == 0 else cell < cells - 1
            raw = h_ref[side, c]
            h_ref[side, c] = jnp.where(column[1] == 0.0, raw, wall) * jnp.where(inside, 1.0, 0.0)

    density = gathered(0)
    w_ref[0:8, :] = jnp.zeros((8, 512), F32)
    w_ref[1032:1040, :] = jnp.zeros((8, 512), F32)

    def walled(rows):
        def body(t, _):
            for u in rows:
                x = t * 16 + u
                at = pl.ds(pl.multiple_of(x * 8, 8), 8)
                kind = jnp.concatenate([t_ref[at, :]] * 4, axis=1)
                dense = jnp.sum(jnp.where(lane == x, density, 0.0), axis=1, keepdims=True)
                wall = dense * jnp.where(kind == 1.0, still, moving)
                w = jnp.where(kind == 0.0, d_ref[at, :], wall)
                w_ref[pl.ds(pl.multiple_of(x * 8 + 8, 8), 8), :] = w
            return 0

        lax.fori_loop(0, GROUP, body, 0)

    depth = lax.broadcasted_iota(jnp.int32, (8, 512), 0)

    def transport(peer, c, out_ref, *place):
        for u in range(ROWS):
            x = peer * 16 + c * ROWS + u
            low = w_ref[pl.ds(pl.multiple_of(x * 8, 8), 8), :]
            w = w_ref[pl.ds(pl.multiple_of(x * 8 + 8, 8), 8), :]
            high = w_ref[pl.ds(pl.multiple_of(x * 8 + 16, 8), 8), :]
            left = jnp.where(depth == 0, h_ref[0, c, pl.ds(peer * ROWS + u, 1), :], pltpu.roll(w, 1, 0))
            right = jnp.where(depth == 7, h_ref[1, c, pl.ds(peer * ROWS + u, 1), :], pltpu.roll(w, 7, 0))
            flow = row_ref[0:1, :] * (w - low) + row_ref[1:2, :] * (high - w)
            flow = flow + row_ref[2:3, :] * (w - left) + row_ref[3:4, :] * (right - w)
            kind = t_ref[pl.ds(pl.multiple_of(x * 8, 8), 8), :]
            kind = jnp.concatenate([kind] * 4, axis=1)
            out_ref[*place, u * 8 : u * 8 + 8, :] = jnp.where(kind == 0.0, w - courant * flow, w)

    def send(c, s):
        peer = lax.rem(me + s, GROUP)
        return remote(
            moved_ref.at[c, peer], x_ref.at[c, me], send_sem.at[c, s], recv_sem.at[c, s], peer
        )

    for c in range(CHUNKS):
        walled(NEED[c])
        halo(c)

        def part(s, _):
            peer = lax.rem(me + s, GROUP)
            transport(peer, c, moved_ref, c, peer)
            send(c, s).start()
            return 0

        lax.fori_loop(1, GROUP, part, 0)
        transport(me, c, x_ref, c, me)
        if c == 1:
            pack(index_ref, all_ref, mid_ref, hot_ref, k_ref)
    for copy in tables:
        copy.wait()

    def chunk(c, _):
        for s in range(1, GROUP):
            send(c, s).wait_recv()

        def load(i, r, half):
            at = (i % 2) * 256 + half * 128
            return x_ref[c, i // 2, r, at : at + 128]

        spectrum(fr, fi, load, jt_ref, kt_ref, x1_ref, x2_ref, sr_ref, s_ref)
        g_ref[...] = jnp.zeros_like(g_ref)

        def directions(q, _):
            for row in range(N):
                s = s_ref[row]
                both = [
                    (s * k_ref[row, pl.ds(base + CHUNKS * q + t, 1), :]).astype(BF16)
                    for base in (0, 16)
                    for t in range(CHUNKS)
                ]
                kind = 1 if row % 8 == 0 else 0
                o = lax.dot_general(
                    ib_ref[kind], jnp.concatenate(both, axis=0), NT, preferred_element_type=F32
                )
                z_ref[:, row * 16 : row * 16 + 16, :] = o.astype(BF16).reshape(N, 16, 256)
            for i in range(N):
                o = lax.dot_general(ia_ref[...], z_ref[i], NN, preferred_element_type=F32)
                g_ref[i] += o[:, :128] * o[:, 128:]
            return 0

        lax.fori_loop(0, DIRS // CHUNKS, directions, 0)
        for row in range(N):
            one = (s_ref[row] * k_ref[row, 32:33, :]).astype(BF16)
            kind = 1 if row % 8 == 0 else 0
            o = lax.dot_general(
                ib_ref[kind], jnp.concatenate([one] * CHUNKS, axis=0), NT, preferred_element_type=F32
            ).astype(BF16)
            for i in range(N):
                lanes = slice(i % CHUNKS * CELLS, i % CHUNKS * CELLS + CELLS)
                zl_ref[i // CHUNKS, row * 16 : row * 16 + 16, lanes] = o[i * 16 : i * 16 + 16, lanes]
        for t in range(N // CHUNKS):
            o = lax.dot_general(ia_ref[...], zl_ref[t], NN, preferred_element_type=F32)
            l_ref[CHUNKS * t : CHUNKS * t + CHUNKS] = o.T.reshape(CHUNKS, CELLS, 256)
        at = pl.ds(pl.multiple_of(me * 128 + c * CELLS, CELLS), CELLS)
        fluid = jnp.concatenate([t_ref[at, :]] * 2, axis=1) == 0.0

        def finish(peer):
            for h in range(2):
                i = 2 * peer + h
                gain = g_ref[i].T
                gain = sum(gain[t * CELLS : t * CELLS + CELLS] for t in range(CHUNKS))
                x = x_ref[c, peer, :, h * 256 : h * 256 + 256]
                change = gain - x * l_ref[i]
                r_ref[c, peer, :, h * 256 : h * 256 + 256] = jnp.where(
                    fluid, x + collision_timestep * change, x
                )

        for group in ((1, 2, 3), (4, 5, 6, 7)):
            for s in group:
                finish(lax.rem(me + s, GROUP))
            for s in group:
                back(c, s).start()
        finish(me)
        pltpu.make_async_copy(r_ref.at[c, me], out_ref.at[me, c], own_sem.at[c]).start()
        return 0

    def back(c, s):
        peer = lax.rem(me + s, GROUP)
        return remote(
            r_ref.at[c, peer], out_ref.at[me, c], back_send.at[c, s], back_recv.at[c, s], peer
        )

    lax.fori_loop(0, CHUNKS, chunk, 0)
    for c in range(CHUNKS):
        pltpu.make_async_copy(r_ref.at[c, me], out_ref.at[me, c], own_sem.at[c]).wait()
        for s in range(1, GROUP):
            send(c, s).wait_send()
            back(c, s).wait()


def constant_tables():
    fr, fi, ir, ii = line_tables()
    to = lambda t: np.asarray(t, np.float32).astype(BF16)
    tables = (j_table(fr, fi), k_tables(fr, fi), inverse_i_tables(ir, ii), inverse_jk_table(ir, ii))
    return (fr, fi), tuple(to(t) for t in tables), packing_index()


def step(distribution, cell_type, index, profiles, first, second, loss, lines, tables):
    hbm = pl.BlockSpec(memory_space=pl.ANY)
    vmem = pl.BlockSpec(memory_space=pltpu.VMEM)
    dma = pltpu.SemaphoreType.DMA
    return pl.pallas_call(
        functools.partial(step_body, *lines),
        out_shape=jax.ShapeDtypeStruct((GROUP, CHUNKS, CELLS, 512), F32),
        in_specs=[hbm, vmem, vmem] + [hbm] * 3 + [vmem] + [hbm] * 4,
        out_specs=pl.BlockSpec(memory_space=pl.ANY),
        scratch_shapes=[
            pltpu.VMEM((1024, 512), F32),
            pltpu.VMEM((1040, 512), F32),
            pltpu.VMEM((1024, 128), F32),
            pltpu.VMEM((2, CHUNKS, 8 * ROWS, 512), F32),
            pltpu.VMEM((2, CHUNKS, 8 * ROWS, 512), F32),
            pltpu.VMEM((2, 2, 128, 8), F32),
            pltpu.VMEM((16, 128), F32),
            pltpu.VMEM((3, GROUP, 16, 128), F32),
            pltpu.VMEM((8, 512), F32),
            pltpu.VMEM((CHUNKS, GROUP, CELLS, 512), F32),
            pltpu.VMEM((CHUNKS, GROUP, CELLS, 512), F32),
            pltpu.VMEM((CHUNKS, GROUP, CELLS, 512), F32),
            pltpu.VMEM((48, 4096), F32),
            pltpu.VMEM((N, 48, 256), F32),
            pltpu.VMEM((4, 512, 256), BF16),
            pltpu.VMEM((N, 48, 256), F32),
            pltpu.VMEM((512, 512), BF16),
            pltpu.VMEM((4, 256, 512), BF16),
            pltpu.VMEM((2, 256, 256), BF16),
            pltpu.VMEM((256, 256), BF16),
            pltpu.VMEM((9 * CELLS, 512), BF16),
            pltpu.VMEM((512, 9 * CELLS), BF16),
            pltpu.VMEM((N // CHUNKS, 256, 128), BF16),
            pltpu.VMEM((N, CELLS, 256), F32),
            pltpu.VMEM((N // CHUNKS, 256, 128), BF16),
            pltpu.VMEM((N, CELLS, 256), F32),
            pltpu.VMEM((N, 256, 256), BF16),
            pltpu.VMEM((N, 256, 128), F32),
            dma((CHUNKS, GROUP)),
            dma((CHUNKS, GROUP)),
            dma((CHUNKS, GROUP)),
            dma((CHUNKS, GROUP)),
            dma((CHUNKS,)),
            dma((8,)),
            dma((GROUP,)),
            dma((3, GROUP)),
            dma((3, GROUP)),
            dma((2, CHUNKS)),
            dma((2, CHUNKS)),
        ],
        compiler_params=pltpu.CompilerParams(
            vmem_limit_bytes=62 << 20, collective_id=0, has_side_effects=True
        ),
        name="step",
    )(distribution, cell_type, index, profiles, first, second, loss, *tables)


def on_device(lines, tables, index, profiles, distribution, cell_type, first, second, loss):
    done = step(
        distribution.reshape(1024, 512),
        cell_type.T,
        index,
        profiles,
        first,
        second,
        loss.reshape(1, 4096),
        lines,
        tables,
    )
    return done.reshape(distribution.shape)


def solution(mesh):
    lines, tables, index = constant_tables()

    def body(*arguments):
        return on_device(lines, tables, index, cell_rows(), *arguments)

    return jax.shard_map(
        body,
        mesh=mesh,
        in_specs=(P(None, "cell", "vel"), P(None, "cell"), P(), P(), P()),
        out_specs=P(None, "cell", "vel"),
        check_vma=False,
    )
```
